512 devices in a mesh: fluid: 64 (over z, y), sub: 4 (over x), struct: 2 (over core).
Axes of the slice: x: 4, y: 8, z: 8, core: 2. Of those that a mesh axis runs over, the one named last changes fastest.
Arguments:
- velocity: float32 [256, 64, 3, 256], P('fluid', 'sub'), may hold values from -6 to 6
- pressure: float32 [256, 64, 256], P('fluid', 'sub'), may hold values from -6 to 6
- viscosity: float32 [256, 64, 256], P('fluid', 'sub'), may hold values from 0.02 to 0.15
- marker_force: float32 [32768, 3, 128], P(('fluid', 'sub', 'struct')), may hold values from -24 to 24
- marker_offset: float32 [32768, 3, 128], P(('fluid', 'sub', 'struct')), may hold values from 0 to 1
- cell_base: int32 [32768, 3, 128], P(('fluid', 'sub', 'struct')), may hold values from 0 to 253, as said below
- block_slab: int32 [32768, 1], P(('fluid', 'sub', 'struct')), may hold values from 0 to 63; in each aligned block of 64 rows (0 to 63, 64 to 127, ...) at most 2 rows name the same one
Outputs:
- new_velocity: float32 [256, 64, 3, 256], P('fluid', 'sub')
- marker_velocity: float32 [32768, 3, 128], P(('fluid', 'sub', 'struct'))
The draws below stay inside these ranges and needn't reach their ends.
Inputs may be any that keep to these rules, and one draw needn't show every extreme that they name: cell_base[b,0,m] lies in 0 to 3, cell_base[b,1,m] in 0 to 15 and cell_base[b,2,m] in 1 to 253. `block_slab`: within the 64 blocks of one device no slab is named more than 2 times.
All inputs are finite; a program needn't handle non-finite values.
Results may differ from the reference program's by a relative error of at most 0.0034.
Values may be sent and summed in bfloat16 or wider, within the bound.
No kernel may reach another device: no remote copies, remote signals or barrier semaphores. Data moves between devices by JAX's collectives and lax.ppermute only.
A program may use at most 64 MiB of HBM per device.

```python
import math
import jax
import jax.numpy as jnp
import numpy as np
from jax import lax

CX = 4
CY = 16
NZ = 256
M = 128
MB = 64
SLABS = 64
SUBS = 4
PAIR_BLOCKS = 128
CAP = 2
NX = 256
NY = 64
NBLK = 32768


def draw_cell_base(key, part):
    keys = jax.random.split(jax.random.fold_in(key, 7), 3)
    first = jax.random.randint(keys[0], (NBLK, 1, M), 0, CX, dtype=jnp.int32)
    second = jax.random.randint(keys[1], (NBLK, 1, M), 0, CY, dtype=jnp.int32)
    third = jax.random.randint(keys[2], (NBLK, 1, M), 1, NZ - 2, dtype=jnp.int32)
    first = first.at[0, 0, 0].set(0).at[0, 0, 1].set(CX - 1)
    second = second.at[0, 0, 1].set(CY - 1)
    third = third.at[0, 0, 0].set(NZ - 3)
    return jnp.concatenate([first, second, third], axis=1)


def block_levels(own_key, dims, cuts, low, top_value):
    loudness, own = 1.0, jax.random.fold_in(own_key, 6)
    for dim, blocks in cuts:
        heights = jnp.exp(jax.random.uniform(jax.random.fold_in(own, dim), (blocks,), jnp.float32, low / len(cuts), top_value / len(cuts)))
        loudness = loudness * jnp.repeat(heights, dims[dim] // blocks).reshape([-1 if axis == dim else 1 for axis in range(len(dims))])
    return loudness


def deal_out(stream_key, own, number, rows, number_of, top, most, skew):
    ranking = jax.random.permutation(stream_key, number_of)
    crowded, usual = shares(number_of, rows * top, most, skew, True), shares(number_of, rows * top, most, skew, False)
    places = jnp.arange(number_of)

    def named(lengths, rotation):
        used = int((lengths > 0).sum())
        fixed = max(1, used // 4)
        shifted = fixed + (places - fixed + rotation * (used - fixed)) % max(1, number_of - fixed)
        return jnp.zeros((number_of,), jnp.int32).at[ranking[jnp.where(places < fixed, places, shifted)]].set(jnp.asarray(lengths, jnp.int32))

    lengths = jnp.where(number % 4 == 0, named(crowded, number // 4), named(usual, number - number // 4 - 1))
    mixed = jax.random.permutation(jax.random.fold_in(own, 3), number_of)
    donor, sink = mixed[0:number_of // 2 * 2:2], mixed[1:number_of // 2 * 2:2]
    slack = jnp.minimum(lengths[donor] - 1, most - lengths[sink]) // 2
    slack = jnp.where((donor == ranking[0]) | (sink == ranking[0]) | (lengths[sink] == 0), 0, jnp.maximum(slack, 0))
    shifted = jax.random.randint(jax.random.fold_in(own, 4), (number_of // 2,), 0, 1 << 20) % (slack + 1)
    lengths = lengths.at[donor].add(-shifted).at[sink].add(shifted)
    labels = jnp.searchsorted(jnp.cumsum(lengths), jnp.arange(rows * top), side="right").astype(jnp.int32)
    grid = labels.reshape(top, rows).T
    grid = grid[jax.random.permutation(jax.random.fold_in(own, 1), rows)]
    rotation = jax.random.randint(jax.random.fold_in(own, 2), (rows, 1), 0, top)
    return jnp.take_along_axis(grid, (jnp.arange(top)[None, :] + rotation) % top, axis=1)


def shares(count, total, most, lean, full):
    loads = [(1 << 20) // math.isqrt(rank ** lean) + 1 for rank in range(1, count + 1)]
    largest = most if full else min(most, max(-(-total // count), total * loads[0] // sum(loads)))
    least = 1 if total - largest >= count - 1 else 0
    holding, surplus = [largest] + [least] * (count - 1), total - largest - least * (count - 1)
    while surplus > 0:
        candidates = [i for i in range(1, count) if holding[i] < largest] or [i for i in range(1, count) if holding[i] < most]
        pool, remaining = sum([loads[i] for i in candidates]), surplus
        for i in candidates:
            addition = min(most - holding[i], max(1, remaining * loads[i] // pool), surplus)
            holding[i] = holding[i] + addition
            surplus = surplus - addition
    return np.array(holding)


def scatter_about(key, dims, scale, most, cuts=(), kind=jnp.bfloat16):
    loudness = block_levels(key, dims, cuts, -0.22, 0.18) if cuts else 1.0
    values = jax.random.normal(key, dims, jnp.float32) * scale * loudness
    return jnp.minimum(jnp.maximum(values, -most), most).astype(kind)


def setup_inputs(seed: int = 0) -> dict:
    splits = jax.random.split(jax.random.key(seed), 8)
    velocity = scatter_about(splits[0], (NX, NY, 3, NZ), 1.0, 6.0, ((0, 64), (1, 4)), jnp.float32)
    pressure = scatter_about(splits[1], (NX, NY, NZ), 1.0, 6.0, ((0, 64), (1, 4)), jnp.float32)
    viscosity = jnp.clip(jnp.exp(math.log(0.15) - 2.014903 * jax.random.uniform(splits[2], (NX, NY, NZ), jnp.float32) ** block_levels(splits[2], (NX, NY, NZ), ((0, 64), (1, 4)), -0.2, 0.2)), 0.02, 0.15)
    marker_force = scatter_about(splits[3], (NBLK, 3, M), 4.0, 24.0, ((0, 512),), jnp.float32)
    marker_offset = jnp.clip(1.0 * jax.random.uniform(splits[4], (NBLK, 3, M), jnp.float32) ** block_levels(splits[4], (NBLK, 3, M), ((0, 512),), -0.2, 0.2), 0.0, 1.0)
    cell_base = draw_cell_base(jax.random.fold_in(splits[7], 71), 0)
    block_slab_keys = jax.random.split(jax.random.fold_in(splits[6], 1), NBLK // MB)
    block_slab_turns = jax.random.permutation(jax.random.fold_in(splits[6], 3), NBLK // MB)
    block_slab = jax.vmap(lambda own, number: deal_out(jax.random.fold_in(splits[6], 2), own, number, MB, SLABS, 1, CAP, 2))(block_slab_keys, block_slab_turns).reshape((NBLK, 1))
    return dict(velocity=velocity, pressure=pressure, viscosity=viscosity, marker_force=marker_force, marker_offset=marker_offset, cell_base=cell_base, block_slab=block_slab)


neighbour_steps = ((1, 0, 0), (-1, 0, 0), (0, 1, 0), (0, -1, 0), (0, 0, 1), (0, 0, -1))

def kernel_weight(distance):
    inside = jnp.minimum(distance, 1.0)
    beyond = jnp.clip(distance - 1.0, 0.0, 1.0)
    inner = (3.0 - 2.0 * inside + jnp.sqrt(1.0 + 4.0 * inside - 4.0 * inside * inside)) * 0.125
    outer = (3.0 - 2.0 * beyond - jnp.sqrt(1.0 + 4.0 * beyond - 4.0 * beyond * beyond)) * 0.125
    return jnp.where(distance < 1.0, inner, outer)

def offset(array, first, second, third):
    extent_first = array.shape[0] - 2
    extent_second = array.shape[1] - 2
    extent_third = array.shape[-1] - 2
    return array[1 + first:1 + first + extent_first, 1 + second:1 + second + extent_second, ..., 1 + third:1 + third + extent_third]

def momentum(old_pad, force):
    velocity_pad = old_pad[:, :, 0:3]
    pressure_pad = old_pad[:, :, 3]
    viscosity_pad = old_pad[:, :, 4]
    centre = offset(velocity_pad, 0, 0, 0)
    viscosity_centre = offset(viscosity_pad, 0, 0, 0)[:, :, None]
    pressure_centre = offset(pressure_pad, 0, 0, 0)
    viscous = jnp.zeros_like(centre)
    for neighbour in neighbour_steps:
        neighbour_value = offset(velocity_pad, neighbour[0], neighbour[1], neighbour[2])
        face_viscosity = 0.5 * (viscosity_centre + offset(viscosity_pad, neighbour[0], neighbour[1], neighbour[2])[:, :, None])
        viscous = viscous + face_viscosity * (neighbour_value - centre)
    gradient = jnp.stack([offset(pressure_pad, 1, 0, 0) - pressure_centre, offset(pressure_pad, 0, 1, 0) - pressure_centre, offset(pressure_pad, 0, 0, 1) - pressure_centre], axis=2)
    return centre + 0.5 * (viscous - gradient + force)

def through_bfloat(values):
    return lax.optimization_barrier(values.astype(jnp.bfloat16)).astype(jnp.float32)

def reference(velocity, pressure, viscosity, marker_force, marker_offset, cell_base, block_slab):
    total_blocks = marker_force.shape[0]
    block_index = jnp.arange(total_blocks, dtype=jnp.int32)
    owner_sub = block_index // PAIR_BLOCKS % SUBS
    slab_index = block_slab[:, 0]
    global_x = (slab_index * CX)[:, None] + cell_base[:, 0, :]
    global_y = (owner_sub * CY)[:, None] + cell_base[:, 1, :]
    global_z = cell_base[:, 2, :]
    reaches = (-1.0, 0.0, 1.0, 2.0)
    weight_x = [kernel_weight(jnp.abs(reach - marker_offset[:, 0, :])) for reach in reaches]
    weight_y = [kernel_weight(jnp.abs(reach - marker_offset[:, 1, :])) for reach in reaches]
    weight_z = [kernel_weight(jnp.abs(reach - marker_offset[:, 2, :])) for reach in reaches]
    component = jnp.arange(3, dtype=jnp.int32)[None, :, None]
    spread_pad = jnp.zeros((NX + 3, NY + 3, 3, NZ), jnp.float32)
    for index_x in range(4):
        row_x = (global_x + index_x)[:, None, :]
        for index_y in range(4):
            row_y = (global_y + index_y)[:, None, :]
            plane = through_bfloat(weight_x[index_x] * weight_y[index_y])[:, None, :]
            for index_z in range(4):
                depth_cell = (global_z + index_z - 1)[:, None, :]
                loaded = through_bfloat(marker_force * weight_z[index_z][:, None, :])
                spread_pad = spread_pad.at[row_x, row_y, component, depth_cell].add(plane * loaded)
    spread = spread_pad[1:NX + 1, 1:NY + 1]
    stacked = jnp.concatenate([velocity, pressure[:, :, None], viscosity[:, :, None]], axis=2)
    old_pad = jnp.pad(stacked, ((1, 1), (1, 1), (0, 0), (1, 1)))
    fresh = momentum(old_pad, spread)
    rounded = through_bfloat(fresh)
    field_pad = jnp.pad(rounded, ((1, 2), (1, 2), (0, 0), (0, 0)))
    sampled = jnp.zeros(marker_force.shape, jnp.float32)
    for index_x in range(4):
        row_x = (global_x + index_x)[:, None, :]
        for index_y in range(4):
            row_y = (global_y + index_y)[:, None, :]
            plane = (weight_x[index_x] * weight_y[index_y])[:, None, :]
            for index_z in range(4):
                depth_cell = (global_z + index_z - 1)[:, None, :]
                depth_weight = through_bfloat(weight_z[index_z])[:, None, :]
                values = field_pad[row_x, row_y, component, depth_cell]
                sampled = sampled + plane * (values * depth_weight)
    return (fresh, sampled)
```

```python
import math

import jax
import jax.numpy as jnp
from jax import lax
from jax.experimental import pallas as pl
from jax.experimental.pallas import tpu as pltpu
from jax.sharding import PartitionSpec as P

M = 128
NZ = 256
YP = 24
XE = 7
ROWS = XE * 3 * YP
ROWS_PAD = 512
GROUP = 8
PAIR = 2

VMEM = pl.BlockSpec(memory_space=pltpu.VMEM)
SMEM = pl.BlockSpec(memory_space=pltpu.SMEM)


def iota(shape, dim):
    return lax.broadcasted_iota(jnp.int32, shape, dim)


def pack_kernel(blocks, slab_ref, offset_ref, base_ref, force_ref, out_ref, pos_ref, count, coords):
    slots = out_ref.shape[0] // 6
    out_ref[...] = jnp.zeros_like(out_ref)
    coords[...] = base_ref[...].astype(jnp.float32) + offset_ref[...]

    def clear(i, carry):
        count[i] = 0
        return carry

    lax.fori_loop(0, slots // 2, clear, 0)
    for b in range(blocks):
        slab = slab_ref[b]
        place = count[slab]
        count[slab] = place + 1
        slot = slab * 2 + place
        pos_ref[b] = slot
        for j in range(3):
            out_ref[pl.ds(slot * 6 + j, 1), :] = coords[j, b : b + 1, :]
            out_ref[pl.ds(slot * 6 + 3 + j, 1), :] = force_ref[j, b : b + 1, :]


def prepare_weights(load_ref, base_ref, weight_ref):
    rows = load_ref.shape[0]
    step = math.gcd(rows, 64)

    def turn(i, carry):
        at = pl.ds(pl.multiple_of(i * step, step), step)
        place = load_ref[at, :]
        base = jnp.floor(place)
        part = place - base
        root = jnp.sqrt(1.0 + 4.0 * part * (1.0 - part)) * 0.125
        falling = (3.0 - 2.0 * part) * 0.125
        rising = (1.0 + 2.0 * part) * 0.125
        base_ref[at, :] = base.astype(jnp.int32)
        weight_ref[0, at, :] = falling - root
        weight_ref[1, at, :] = falling + root
        weight_ref[2, at, :] = rising + root
        weight_ref[3, at, :] = rising - root
        return carry

    lax.fori_loop(0, rows // step, turn, 0)


def pick(index, weights):
    out = jnp.where(index == 0, weights[0], 0.0)
    for j in range(1, 4):
        out = jnp.where(index == j, weights[j], out)
    return out


def row8(ref, row):
    return jnp.broadcast_to(ref[pl.ds(row, 1), :], (8, M))


def block_weights(base_ref, weight_ref, row, row_x):
    sub = iota((8, M), 0)
    bx = row8(base_ref, row)
    by = row8(base_ref, row + 1)
    bz = row8(base_ref, row + 2)
    wx_in = [row8(weight_ref.at[j], row) for j in range(4)]
    wy_in = [row8(weight_ref.at[j], row + 1) for j in range(4)]
    wz_in = [row8(weight_ref.at[j], row + 2) for j in range(4)]
    row_x[...] = pick(sub - bx, wx_in)
    along_x = [jnp.broadcast_to(row_x[x : x + 1, :], (8, M)) for x in range(XE)]
    cells_y = [
        sub,
        sub + 8,
        jnp.where(sub < 2, sub + 16, jnp.where(sub == 7, -1, -100)),
    ]
    along_y = [pick(cell - by + 1, wy_in) for cell in cells_y]
    lead = sub - bz + 1
    tile = (7 - lead) >> 3
    value = pick(lead & 7, wz_in)
    along_z = jnp.concatenate(
        [jnp.where(tile == r, value, 0.0) for r in range(NZ // 8)], axis=0
    ).astype(jnp.bfloat16)
    return along_x, along_y, along_z


def spread_kernel(load_ref, out_ref, base_ref, weight_ref, row_x, left, right, total):
    blocks = load_ref.shape[0] // 6
    prepare_weights(load_ref, base_ref, weight_ref)
    total[...] = jnp.zeros_like(total)

    def turn(i, carry):
        for g in range(GROUP):
            row = (i * GROUP + g) * 6
            along_x, along_y, along_z = block_weights(base_ref, weight_ref, row, row_x.at[g])
            right[:, g * M : (g + 1) * M] = along_z
            force = [row8(load_ref, row + 3 + c) for c in range(3)]
            tiles = []
            for x in range(XE):
                for c in range(3):
                    push = along_x[x] * force[c]
                    tiles += [push * along_y[k] for k in range(3)]
            tiles.append(jnp.zeros((8, M), jnp.float32))
            left[:, g * M : (g + 1) * M] = jnp.concatenate(tiles, axis=0).astype(jnp.bfloat16)
        total[...] += lax.dot_general(
            left[...], right[...], (((1,), (1,)), ((), ())), preferred_element_type=jnp.float32
        )
        return carry

    lax.fori_loop(0, blocks // GROUP, turn, 0)
    out_ref[...] = total[...].astype(out_ref.dtype)


def join_kernel(mine_ref, other_ref, old_ref, sum_ref, low_ref, high_ref):
    rim = 9 * YP
    sum_ref[...] = 0.5 * (
        mine_ref[0:ROWS, :].astype(jnp.float32) + other_ref[0:ROWS, :].astype(jnp.float32)
    )
    for x in range(4):
        for c in range(3):
            at = ((x + 1) * 3 + c) * YP
            sum_ref[at : at + 16, :] += old_ref[x, c]
    low_ref[...] = sum_ref[0:rim, :].astype(jnp.bfloat16)
    high_ref[...] = sum_ref[ROWS - rim : ROWS, :].astype(jnp.bfloat16)


HIGH_ROWS = (15, 16, 17)
LOW_ROWS = (23, 0, 1)


def fold_kernel(sum_ref, left_ref, right_ref, out_ref, low_ref, high_ref, low, high):
    rim = 9 * YP
    out_ref[rim : ROWS - rim, :] = sum_ref[rim : ROWS - rim, :]
    out_ref[0:rim, :] = sum_ref[0:rim, :] + left_ref[...].astype(jnp.float32)
    out_ref[ROWS - rim : ROWS, :] = sum_ref[ROWS - rim : ROWS, :] + right_ref[...].astype(jnp.float32)
    low[...] = jnp.zeros_like(low)
    high[...] = jnp.zeros_like(high)
    for g in range(XE * 3):
        for j in range(3):
            lanes = slice(j * NZ, (j + 1) * NZ)
            low[g : g + 1, lanes] = out_ref[g * YP + LOW_ROWS[j] : g * YP + LOW_ROWS[j] + 1, :]
            high[g : g + 1, lanes] = out_ref[g * YP + HIGH_ROWS[j] : g * YP + HIGH_ROWS[j] + 1, :]
    low_ref[...] = low[...].astype(jnp.bfloat16)
    high_ref[...] = high[...].astype(jnp.bfloat16)


def sample_kernel(
    fluid_count,
    sub_count,
    place_ref,
    load_ref,
    sum_ref,
    below_ref,
    above_ref,
    fresh_ref,
    out_ref,
    base_ref,
    weight_ref,
    row_x,
    grid,
    field,
    below,
    above,
):
    blocks = load_ref.shape[0] // 6
    prepare_weights(load_ref, base_ref, weight_ref)
    grid[...] = sum_ref[...]
    below[...] = below_ref[...].astype(jnp.float32)
    above[...] = above_ref[...].astype(jnp.float32)
    for g in range(XE * 3):
        for j in range(3):
            lanes = slice(j * NZ, (j + 1) * NZ)
            at = g * YP + LOW_ROWS[j]
            grid[at : at + 1, :] += below[g : g + 1, lanes]
            at = g * YP + HIGH_ROWS[j]
            grid[at : at + 1, :] += above[g : g + 1, lanes]
    for x in range(4):
        for c in range(3):
            at = ((x + 1) * 3 + c) * YP
            fresh_ref[x, c] = grid[at : at + 16, :]
    first = place_ref[0]
    second = place_ref[1]
    sub = iota((8, NZ), 0)
    inside = ((sub < 2) & (second < sub_count - 1)) | ((sub == 7) & (second > 0))
    for g in range(XE * 3):
        at = g * YP + 16
        grid[at : at + 8, :] = jnp.where(inside, grid[at : at + 8, :], 0.0)
    rim = 3 * YP

    @pl.when(first == 0)
    def _():
        grid[0:rim, :] = jnp.zeros((rim, NZ), jnp.float32)

    @pl.when(first == fluid_count - 1)
    def _():
        grid[5 * rim : ROWS, :] = jnp.zeros((2 * rim, NZ), jnp.float32)

    field[0:ROWS, :] = grid[...].astype(jnp.bfloat16)
    field[ROWS:ROWS_PAD, :] = jnp.zeros((ROWS_PAD - ROWS, NZ), jnp.bfloat16)

    def turn(i, carry):
        parts = []
        zs = []
        for g in range(PAIR):
            row = (i * PAIR + g) * 6
            along_x, along_y, along_z = block_weights(base_ref, weight_ref, row, row_x.at[g])
            parts.append((along_x, along_y))
            zs.append(along_z)
        seen = lax.dot_general(
            field[...],
            jnp.concatenate(zs, axis=1),
            (((1,), (0,)), ((), ())),
            preferred_element_type=jnp.float32,
        )
        for g in range(PAIR):
            along_x, along_y = parts[g]
            sums = [jnp.zeros((8, M), jnp.float32) for _ in range(3)]
            for x in range(XE):
                for k in range(3):
                    plane = along_x[x] * along_y[k]
                    for c in range(3):
                        at = (x * 3 + c) * YP + k * 8
                        sums[c] = sums[c] + plane * seen[at : at + 8, g * M : (g + 1) * M]
            for c in range(3):
                out_ref[pl.ds((i * PAIR + g) * 3 + c, 1), :] = jnp.sum(
                    sums[c], axis=0, keepdims=True
                )
        return carry

    lax.fori_loop(0, blocks // PAIR, turn, 0)


def take_kernel(blocks, pos_ref, in_ref, out_ref):
    for b in range(blocks):
        slot = pos_ref[b]
        for c in range(3):
            out_ref[c, b : b + 1, :] = in_ref[pl.ds(slot * 3 + c, 1), :]


def shift(array, axis, by):
    count = lax.axis_size(axis)
    if by > 0:
        pairs = [(i, i + 1) for i in range(count - 1)]
    else:
        pairs = [(i + 1, i) for i in range(count - 1)]
    return lax.ppermute(array, axis, pairs)


def old_part(velocity, pressure, viscosity):
    v = jnp.transpose(velocity, (0, 2, 1, 3))
    p = pressure[:, None]
    n = viscosity[:, None]
    every = jnp.concatenate([v, p, n], axis=1)
    before_x = shift(every[-1:], "fluid", 1)
    after_x = shift(every[:1], "fluid", -1)
    before_y = shift(every[:, :, -1:], "sub", 1)
    after_y = shift(every[:, :, :1], "sub", -1)
    zero = jnp.zeros_like(every[..., :1])
    around = (
        jnp.concatenate([every[1:], after_x], axis=0),
        jnp.concatenate([before_x, every[:-1]], axis=0),
        jnp.concatenate([every[:, :, 1:], after_y], axis=2),
        jnp.concatenate([before_y, every[:, :, :-1]], axis=2),
        jnp.concatenate([every[..., 1:], zero], axis=3),
        jnp.concatenate([zero, every[..., :-1]], axis=3),
    )
    viscous = jnp.zeros_like(v)
    for near in around:
        viscous = viscous + 0.5 * (n + near[:, 4:5]) * (near[:, 0:3] - v)
    gradient = jnp.concatenate([around[k][:, 3:4] - p for k in (0, 2, 4)], axis=1)
    return v + 0.5 * (viscous - gradient)


def kernel_params():
    return pltpu.CompilerParams(vmem_limit_bytes=60 * 1024 * 1024)


def body(velocity, pressure, viscosity, marker_force, marker_offset, cell_base, block_slab):
    f32, bf16 = jnp.float32, jnp.bfloat16
    shape = jax.ShapeDtypeStruct
    blocks = marker_force.shape[0]
    slabs = lax.axis_size("fluid")
    subs = lax.axis_size("sub")
    slots = 2 * slabs
    swap01 = lambda array: jnp.transpose(array, (1, 0, 2))
    payload, position = pl.pallas_call(
        lambda *refs: pack_kernel(blocks, *refs),
        out_shape=(shape((slots * 6, M), f32), shape((blocks,), jnp.int32)),
        in_specs=[SMEM, VMEM, VMEM, VMEM],
        out_specs=(VMEM, SMEM),
        scratch_shapes=[pltpu.SMEM((slabs,), jnp.int32), pltpu.VMEM((3, blocks, M), f32)],
        name="pack",
    )(block_slab[:, 0], swap01(marker_offset), swap01(cell_base), swap01(marker_force))
    arrived = lax.all_to_all(
        payload.reshape(slabs, 3, 4, M), "fluid", split_axis=0, concat_axis=0, tiled=True
    ).reshape(slots * 6, M)
    old = old_part(velocity, pressure, viscosity)
    partial_grid = pl.pallas_call(
        spread_kernel,
        out_shape=shape((ROWS_PAD, NZ), bf16),
        in_specs=[VMEM],
        out_specs=VMEM,
        scratch_shapes=[
            pltpu.VMEM((slots * 6, M), jnp.int32),
            pltpu.VMEM((4, slots * 6, M), f32),
            pltpu.VMEM((GROUP, 8, M), f32),
            pltpu.VMEM((ROWS_PAD, GROUP * M), bf16),
            pltpu.VMEM((NZ, GROUP * M), bf16),
            pltpu.VMEM((ROWS_PAD, NZ), f32),
        ],
        compiler_params=kernel_params(),
        name="spread",
    )(arrived)
    other_grid = lax.ppermute(partial_grid, "struct", [(0, 1), (1, 0)])
    rim = 9 * YP
    summed, low, high = pl.pallas_call(
        join_kernel,
        out_shape=(shape((ROWS, NZ), f32), shape((rim, NZ), bf16), shape((rim, NZ), bf16)),
        in_specs=[VMEM] * 3,
        out_specs=(VMEM,) * 3,
        name="join",
    )(partial_grid, other_grid, old)
    from_left = shift(high, "fluid", 1)
    from_right = shift(low, "fluid", -1)
    folded, low, high = pl.pallas_call(
        fold_kernel,
        out_shape=(shape((ROWS, NZ), f32), shape((24, 3 * NZ), bf16), shape((24, 3 * NZ), bf16)),
        in_specs=[VMEM] * 3,
        out_specs=(VMEM,) * 3,
        scratch_shapes=[pltpu.VMEM((24, 3 * NZ), f32)] * 2,
        name="fold",
    )(summed, from_left, from_right)
    from_below = shift(high, "sub", 1)
    from_above = shift(low, "sub", -1)
    place = jnp.stack([lax.axis_index("fluid"), lax.axis_index("sub")]).astype(jnp.int32)
    fresh, sampled = pl.pallas_call(
        lambda *refs: sample_kernel(slabs, subs, *refs),
        out_shape=(shape((4, 3, 16, NZ), f32), shape((slots * 3, M), f32)),
        in_specs=[SMEM] + [VMEM] * 4,
        out_specs=(VMEM, VMEM),
        scratch_shapes=[
            pltpu.VMEM((slots * 6, M), jnp.int32),
            pltpu.VMEM((4, slots * 6, M), f32),
            pltpu.VMEM((PAIR, 8, M), f32),
            pltpu.VMEM((ROWS, NZ), f32),
            pltpu.VMEM((ROWS_PAD, NZ), bf16),
            pltpu.VMEM((24, 3 * NZ), f32),
            pltpu.VMEM((24, 3 * NZ), f32),
        ],
        compiler_params=kernel_params(),
        name="sample",
    )(place, arrived, folded, from_below, from_above)
    returned = lax.all_to_all(
        sampled.reshape(slabs, 3, 2, M), "fluid", split_axis=0, concat_axis=0, tiled=True
    ).reshape(slots * 3, M)
    result = pl.pallas_call(
        lambda *refs: take_kernel(blocks, *refs),
        out_shape=shape((3, blocks, M), f32),
        in_specs=[SMEM, VMEM],
        out_specs=VMEM,
        name="take",
    )(position, returned)
    return (jnp.transpose(fresh, (0, 2, 1, 3)), swap01(result))


def solution(mesh):
    return jax.shard_map(
        body,
        mesh=mesh,
        in_specs=(
            P("fluid", "sub", None, None),
            P("fluid", "sub", None),
            P("fluid", "sub", None),
            P(("fluid", "sub", "struct"), None, None),
            P(("fluid", "sub", "struct"), None, None),
            P(("fluid", "sub", "struct"), None, None),
            P(("fluid", "sub", "struct"), None),
        ),
        out_specs=(P("fluid", "sub", None, None), P(("fluid", "sub", "struct"), None, None)),
        check_vma=False,
    )
```

```python
import math

import jax
import jax.numpy as jnp
from jax import lax
from jax.experimental import pallas as pl
from jax.experimental.pallas import tpu as pltpu
from jax.sharding import PartitionSpec as P

M = 128
NZ = 256
YP = 24
XE = 7
ROWS = XE * YP
ROWS_PAD = 176
FIELD = 512
GROUP = 32
PAIR = 2
TURNS = 16

VMEM = pl.BlockSpec(memory_space=pltpu.VMEM)
SMEM = pl.BlockSpec(memory_space=pltpu.SMEM)


def iota(shape, dim):
    return lax.broadcasted_iota(jnp.int32, shape, dim)


def pack_kernel(blocks, slab_ref, offset_ref, base_ref, force_ref, out_ref, pos_ref, count, coords):
    slots = out_ref.shape[0] // 6
    out_ref[...] = jnp.zeros_like(out_ref)
    coords[...] = base_ref[...].astype(jnp.float32) + offset_ref[...]

    def clear(i, carry):
        count[i] = 0
        return carry

    lax.fori_loop(0, slots // 2, clear, 0)
    for b in range(blocks):
        slab = slab_ref[b]
        place = count[slab]
        count[slab] = place + 1
        slot = slab * 2 + place
        pos_ref[b] = slot
        for j in range(3):
            out_ref[pl.ds(slot * 6 + j, 1), :] = coords[j, b : b + 1, :]
            out_ref[pl.ds(slot * 6 + 3 + j, 1), :] = force_ref[j, b : b + 1, :]


def prepare_weights(load_ref, base_ref, weight_ref):
    rows = load_ref.shape[0]
    step = math.gcd(rows, 64)

    def turn(i, carry):
        at = pl.ds(pl.multiple_of(i * step, step), step)
        place = load_ref[at, :]
        base = jnp.floor(place)
        part = place - base
        root = jnp.sqrt(1.0 + 4.0 * part * (1.0 - part)) * 0.125
        falling = (3.0 - 2.0 * part) * 0.125
        rising = (1.0 + 2.0 * part) * 0.125
        base_ref[at, :] = base.astype(jnp.int32)
        weight_ref[0, at, :] = falling - root
        weight_ref[1, at, :] = falling + root
        weight_ref[2, at, :] = rising + root
        weight_ref[3, at, :] = rising - root
        return carry

    lax.fori_loop(0, rows // step, turn, 0)


def pick(index, weights):
    out = jnp.where(index == 0, weights[0], 0.0)
    for j in range(1, 4):
        out = jnp.where(index == j, weights[j], out)
    return out


def row8(ref, row):
    return jnp.broadcast_to(ref[pl.ds(row, 1), :], (8, M))


def block_weights(base_ref, weight_ref, row, row_x):
    sub = iota((8, M), 0)
    bx = row8(base_ref, row)
    by = row8(base_ref, row + 1)
    bz = row8(base_ref, row + 2)
    wx_in = [row8(weight_ref.at[j], row) for j in range(4)]
    wy_in = [row8(weight_ref.at[j], row + 1) for j in range(4)]
    wz_in = [row8(weight_ref.at[j], row + 2) for j in range(4)]
    row_x[...] = pick(sub - bx, wx_in)
    along_x = [jnp.broadcast_to(row_x[x : x + 1, :], (8, M)) for x in range(XE)]
    cells_y = [
        sub + 1,
        sub + 9,
        jnp.where(sub < 2, sub + 17, jnp.where(sub == 7, 0, -100)),
    ]
    along_y = [pick(cell - by, wy_in) for cell in cells_y]
    tiles = []
    values = []
    for half in range(2):
        lead = sub - bz + (1 + 8 * half)
        tiles.append(((15 - lead) >> 4).astype(jnp.float32))
        values.append(pick(lead & 15, wz_in))
    tile = jnp.concatenate(tiles, axis=0).astype(jnp.bfloat16)
    return along_x, along_y, tile, values


def expand(tile, value):
    zero = jnp.zeros((16, M), jnp.bfloat16)
    value = jnp.concatenate(value, axis=0).astype(jnp.bfloat16)
    return [jnp.where(tile == r, value, zero) for r in range(NZ // 16)]


def spread_kernel(load_ref, out_ref, base_ref, weight_ref, row_x, total):
    blocks = load_ref.shape[0] // 6
    prepare_weights(load_ref, base_ref, weight_ref)
    total[...] = jnp.zeros_like(total)

    def turn(i, carry):
        planes = []
        loads = []
        for g in range(GROUP):
            row = (i * GROUP + g) * 6
            along_x, along_y, tile, value = block_weights(
                base_ref, weight_ref, row, row_x.at[g]
            )
            loaded = []
            for c in range(3):
                force = row8(load_ref, row + 3 + c)
                loaded += expand(tile, [part * force for part in value])
            loads.append(jnp.concatenate(loaded, axis=0))
            plane = [along_x[x] * along_y[k] for x in range(XE) for k in range(3)]
            plane.append(jnp.zeros((8, M), jnp.float32))
            planes.append(jnp.concatenate(plane, axis=0).astype(jnp.bfloat16))
        total[...] += lax.dot_general(
            jnp.concatenate(loads, axis=1),
            jnp.concatenate(planes, axis=1),
            (((1,), (1,)), ((), ())),
            preferred_element_type=jnp.float32,
        )
        return carry

    lax.fori_loop(0, blocks // GROUP, turn, 0)
    out_ref[...] = jnp.transpose(total[...]).astype(out_ref.dtype)


def join_kernel(mine_ref, other_ref, old_ref, sum_ref, low_ref, high_ref):
    rim = 3 * YP
    sum_ref[...] = 0.5 * (
        mine_ref[0:ROWS, :].astype(jnp.float32) + other_ref[0:ROWS, :].astype(jnp.float32)
    )
    for x in range(4):
        for c in range(3):
            at = (x + 1) * YP
            sum_ref[at : at + 16, c * NZ : (c + 1) * NZ] += old_ref[x, c]
    low_ref[...] = sum_ref[0:rim, :].astype(jnp.bfloat16)
    high_ref[...] = sum_ref[ROWS - rim : ROWS, :].astype(jnp.bfloat16)


HIGH_ROWS = (15, 16, 17)
LOW_ROWS = (23, 0, 1)


def fold_kernel(sum_ref, left_ref, right_ref, out_ref, low_ref, high_ref, low, high):
    rim = 3 * YP
    out_ref[rim : ROWS - rim, :] = sum_ref[rim : ROWS - rim, :]
    out_ref[0:rim, :] = sum_ref[0:rim, :] + left_ref[...].astype(jnp.float32)
    out_ref[ROWS - rim : ROWS, :] = sum_ref[ROWS - rim : ROWS, :] + right_ref[...].astype(jnp.float32)
    low[...] = jnp.zeros_like(low)
    high[...] = jnp.zeros_like(high)
    for x in range(XE):
        for j in range(3):
            to = x * 3 + j
            at = x * YP + LOW_ROWS[j]
            low[to : to + 1, :] = out_ref[at : at + 1, :]
            at = x * YP + HIGH_ROWS[j]
            high[to : to + 1, :] = out_ref[at : at + 1, :]
    low_ref[...] = low[...].astype(jnp.bfloat16)
    high_ref[...] = high[...].astype(jnp.bfloat16)


def sample_kernel(
    fluid_count,
    sub_count,
    place_ref,
    load_ref,
    sum_ref,
    below_ref,
    above_ref,
    fresh_ref,
    out_ref,
    base_ref,
    weight_ref,
    row_x,
    grid,
    field,
    below,
    above,
):
    blocks = load_ref.shape[0] // 6
    prepare_weights(load_ref, base_ref, weight_ref)
    grid[...] = sum_ref[...]
    below[...] = below_ref[...].astype(jnp.float32)
    above[...] = above_ref[...].astype(jnp.float32)
    for x in range(XE):
        for j in range(3):
            come = x * 3 + j
            at = x * YP + LOW_ROWS[j]
            grid[at : at + 1, :] += below[come : come + 1, :]
            at = x * YP + HIGH_ROWS[j]
            grid[at : at + 1, :] += above[come : come + 1, :]
    for x in range(4):
        for c in range(3):
            at = (x + 1) * YP
            fresh_ref[x, c] = grid[at : at + 16, c * NZ : (c + 1) * NZ]
    first = place_ref[0]
    second = place_ref[1]
    sub = iota((8, 3 * NZ), 0)
    inside = ((sub < 2) & (second < sub_count - 1)) | ((sub == 7) & (second > 0))
    for x in range(XE):
        at = x * YP + 16
        grid[at : at + 8, :] = jnp.where(inside, grid[at : at + 8, :], 0.0)

    @pl.when(first == 0)
    def _():
        grid[0:YP, :] = jnp.zeros((YP, 3 * NZ), jnp.float32)

    @pl.when(first == fluid_count - 1)
    def _():
        grid[5 * YP : ROWS, :] = jnp.zeros((2 * YP, 3 * NZ), jnp.float32)

    rows = [grid[:, c * NZ : (c + 1) * NZ] for c in range(3)]
    rows.append(jnp.zeros((FIELD - 3 * ROWS, NZ), jnp.float32))
    field[...] = jnp.concatenate(rows, axis=0).astype(jnp.bfloat16)

    def turn(i, carry):
        for t in range(TURNS):
            block = (i * TURNS + t) * PAIR
            parts = []
            depth = []
            for g in range(PAIR):
                along_x, along_y, tile, value = block_weights(
                    base_ref, weight_ref, (block + g) * 6, row_x.at[t * PAIR + g]
                )
                parts.append((along_x, along_y))
                depth.append(jnp.concatenate(expand(tile, value), axis=0))
            seen = lax.dot_general(
                field[...],
                jnp.concatenate(depth, axis=1),
                (((1,), (0,)), ((), ())),
                preferred_element_type=jnp.float32,
            )
            for g in range(PAIR):
                along_x, along_y = parts[g]
                for c in range(3):
                    total = 0.0
                    for k in range(3):
                        inner = 0.0
                        for x in range(XE):
                            at = c * ROWS + x * YP + k * 8
                            inner = inner + along_x[x] * seen[at : at + 8, g * M : (g + 1) * M]
                        total = total + inner * along_y[k]
                    out_ref[pl.ds((block + g) * 3 + c, 1), :] = jnp.sum(
                        total, axis=0, keepdims=True
                    )
        return carry

    lax.fori_loop(0, blocks // (PAIR * TURNS), turn, 0)


def take_kernel(blocks, pos_ref, in_ref, out_ref):
    for b in range(blocks):
        slot = pos_ref[b]
        for c in range(3):
            out_ref[c, b : b + 1, :] = in_ref[pl.ds(slot * 3 + c, 1), :]


def shift(array, axis, by):
    count = lax.axis_size(axis)
    if by > 0:
        pairs = [(i, i + 1) for i in range(count - 1)]
    else:
        pairs = [(i + 1, i) for i in range(count - 1)]
    return lax.ppermute(array, axis, pairs)


def old_part(velocity, pressure, viscosity):
    v = jnp.transpose(velocity, (0, 2, 1, 3))
    p = pressure[:, None]
    n = viscosity[:, None]
    every = jnp.concatenate([v, p, n], axis=1)
    before_x = shift(every[-1:], "fluid", 1)
    after_x = shift(every[:1], "fluid", -1)
    before_y = shift(every[:, :, -1:], "sub", 1)
    after_y = shift(every[:, :, :1], "sub", -1)
    zero = jnp.zeros_like(every[..., :1])
    around = (
        jnp.concatenate([every[1:], after_x], axis=0),
        jnp.concatenate([before_x, every[:-1]], axis=0),
        jnp.concatenate([every[:, :, 1:], after_y], axis=2),
        jnp.concatenate([before_y, every[:, :, :-1]], axis=2),
        jnp.concatenate([every[..., 1:], zero], axis=3),
        jnp.concatenate([zero, every[..., :-1]], axis=3),
    )
    viscous = jnp.zeros_like(v)
    for near in around:
        viscous = viscous + 0.5 * (n + near[:, 4:5]) * (near[:, 0:3] - v)
    gradient = jnp.concatenate([around[k][:, 3:4] - p for k in (0, 2, 4)], axis=1)
    return v + 0.5 * (viscous - gradient)


def grant(mib):
    return pltpu.CompilerParams(vmem_limit_bytes=mib * 1024 * 1024)


def spread(arrived):
    return pl.pallas_call(
        spread_kernel,
        out_shape=jax.ShapeDtypeStruct((ROWS_PAD, 3 * NZ), jnp.bfloat16),
        in_specs=[VMEM],
        out_specs=VMEM,
        scratch_shapes=[
            pltpu.VMEM(arrived.shape, jnp.int32),
            pltpu.VMEM((4, *arrived.shape), jnp.float32),
            pltpu.VMEM((GROUP, 8, M), jnp.float32),
            pltpu.VMEM((3 * NZ, ROWS_PAD), jnp.float32),
        ],
        compiler_params=grant(16),
        name="spread",
    )(arrived)


def sample(slabs, subs, place, arrived, folded, from_below, from_above):
    lanes = 3 * NZ
    return pl.pallas_call(
        lambda *refs: sample_kernel(slabs, subs, *refs),
        out_shape=(
            jax.ShapeDtypeStruct((4, 3, 16, NZ), jnp.float32),
            jax.ShapeDtypeStruct((arrived.shape[0] // 2, M), jnp.float32),
        ),
        in_specs=[SMEM] + [VMEM] * 4,
        out_specs=(VMEM, VMEM),
        scratch_shapes=[
            pltpu.VMEM(arrived.shape, jnp.int32),
            pltpu.VMEM((4, *arrived.shape), jnp.float32),
            pltpu.VMEM((PAIR * TURNS, 8, M), jnp.float32),
            pltpu.VMEM((ROWS, lanes), jnp.float32),
            pltpu.VMEM((FIELD, NZ), jnp.bfloat16),
            pltpu.VMEM((24, lanes), jnp.float32),
            pltpu.VMEM((24, lanes), jnp.float32),
        ],
        compiler_params=grant(16),
        name="sample",
    )(place, arrived, folded, from_below, from_above)


def body(velocity, pressure, viscosity, marker_force, marker_offset, cell_base, block_slab):
    f32, bf16 = jnp.float32, jnp.bfloat16
    shape = jax.ShapeDtypeStruct
    blocks = marker_force.shape[0]
    slabs = lax.axis_size("fluid")
    subs = lax.axis_size("sub")
    slots = 2 * slabs
    lanes = 3 * NZ
    swap01 = lambda array: jnp.transpose(array, (1, 0, 2))
    payload, position = pl.pallas_call(
        lambda *refs: pack_kernel(blocks, *refs),
        out_shape=(shape((slots * 6, M), f32), shape((blocks,), jnp.int32)),
        in_specs=[SMEM, VMEM, VMEM, VMEM],
        out_specs=(VMEM, SMEM),
        scratch_shapes=[pltpu.SMEM((slabs,), jnp.int32), pltpu.VMEM((3, blocks, M), f32)],
        compiler_params=grant(60),
        name="pack",
    )(block_slab[:, 0], swap01(marker_offset), swap01(cell_base), swap01(marker_force))
    payload, velocity, pressure, viscosity = lax.optimization_barrier(
        (payload, velocity, pressure, viscosity)
    )
    arrived = lax.all_to_all(
        payload.reshape(slabs, 3, 4, M), "fluid", split_axis=0, concat_axis=0, tiled=True
    ).reshape(slots * 6, M)
    old = old_part(velocity, pressure, viscosity)
    partial_grid = spread(arrived)
    other_grid = lax.ppermute(partial_grid, "struct", [(0, 1), (1, 0)])
    rim = 3 * YP
    summed, low, high = pl.pallas_call(
        join_kernel,
        out_shape=(shape((ROWS, lanes), f32), shape((rim, lanes), bf16), shape((rim, lanes), bf16)),
        in_specs=[VMEM] * 3,
        out_specs=(VMEM,) * 3,
        compiler_params=grant(6),
        name="join",
    )(partial_grid, other_grid, old)
    from_left = shift(high, "fluid", 1)
    from_right = shift(low, "fluid", -1)
    folded, low, high = pl.pallas_call(
        fold_kernel,
        out_shape=(shape((ROWS, lanes), f32), shape((24, lanes), bf16), shape((24, lanes), bf16)),
        in_specs=[VMEM] * 3,
        out_specs=(VMEM,) * 3,
        scratch_shapes=[pltpu.VMEM((24, lanes), f32)] * 2,
        compiler_params=grant(6),
        name="fold",
    )(summed, from_left, from_right)
    from_below = shift(high, "sub", 1)
    from_above = shift(low, "sub", -1)
    place = jnp.stack([lax.axis_index("fluid"), lax.axis_index("sub")]).astype(jnp.int32)
    fresh, sampled = sample(slabs, subs, place, arrived, folded, from_below, from_above)
    returned = lax.all_to_all(
        sampled.reshape(slabs, 3, 2, M), "fluid", split_axis=0, concat_axis=0, tiled=True
    ).reshape(slots * 3, M)
    result = pl.pallas_call(
        lambda *refs: take_kernel(blocks, *refs),
        out_shape=shape((3, blocks, M), f32),
        in_specs=[SMEM, VMEM],
        out_specs=VMEM,
        compiler_params=grant(2),
        name="take",
    )(position, returned)
    return (jnp.transpose(fresh, (0, 2, 1, 3)), swap01(result))


def solution(mesh):
    return jax.shard_map(
        body,
        mesh=mesh,
        in_specs=(
            P("fluid", "sub", None, None),
            P("fluid", "sub", None),
            P("fluid", "sub", None),
            P(("fluid", "sub", "struct"), None, None),
            P(("fluid", "sub", "struct"), None, None),
            P(("fluid", "sub", "struct"), None, None),
            P(("fluid", "sub", "struct"), None),
        ),
        out_specs=(P("fluid", "sub", None, None), P(("fluid", "sub", "struct"), None, None)),
        check_vma=False,
    )
```

```python
import math

import jax
import jax.numpy as jnp
from jax import lax
from jax.experimental import pallas as pl
from jax.experimental.pallas import tpu as pltpu
from jax.sharding import PartitionSpec as P

M = 128
NZ = 256
YP = 24
XE = 7
ROWS = XE * YP
ROWS_PAD = 176
FIELD = 512
GROUP = 32
PAIR = 2
TURNS = 16

VMEM = pl.BlockSpec(memory_space=pltpu.VMEM)
SMEM = pl.BlockSpec(memory_space=pltpu.SMEM)


def iota(shape, dim):
    return lax.broadcasted_iota(jnp.int32, shape, dim)


def pack_kernel(blocks, slab_ref, offset_ref, base_ref, force_ref, out_ref, pos_ref, count, coords):
    slots = out_ref.shape[0] // 6
    out_ref[...] = jnp.zeros_like(out_ref)
    coords[...] = base_ref[...].astype(jnp.float32) + offset_ref[...]

    for i in range(slots // 2):
        count[i] = 0
    for b in range(blocks):
        slab = slab_ref[b]
        place = count[slab]
        count[slab] = place + 1
        slot = slab * 2 + place
        pos_ref[b] = slot
        for j in range(3):
            out_ref[pl.ds(slot * 6 + j, 1), :] = coords[j, b : b + 1, :]
            out_ref[pl.ds(slot * 6 + 3 + j, 1), :] = force_ref[j, b : b + 1, :]


def prepare_weights(load_ref, base_ref, weight_ref):
    rows = load_ref.shape[0]
    step = math.gcd(rows, 64)

    def turn(i, carry):
        at = pl.ds(pl.multiple_of(i * step, step), step)
        place = load_ref[at, :]
        base = jnp.floor(place)
        part = place - base
        root = jnp.sqrt(1.0 + 4.0 * part * (1.0 - part)) * 0.125
        falling = (3.0 - 2.0 * part) * 0.125
        rising = (1.0 + 2.0 * part) * 0.125
        base_ref[at, :] = base.astype(jnp.int32)
        weight_ref[0, at, :] = falling - root
        weight_ref[1, at, :] = falling + root
        weight_ref[2, at, :] = rising + root
        weight_ref[3, at, :] = rising - root
        return carry

    lax.fori_loop(0, rows // step, turn, 0)


def pick(index, weights):
    out = jnp.where(index == 0, weights[0], 0.0)
    for j in range(1, 4):
        out = jnp.where(index == j, weights[j], out)
    return out


def row8(ref, row):
    return jnp.broadcast_to(ref[pl.ds(row, 1), :], (8, M))


def block_weights(base_ref, weight_ref, row, row_x):
    sub = iota((8, M), 0)
    bx = row8(base_ref, row)
    by = row8(base_ref, row + 1)
    bz = row8(base_ref, row + 2)
    wx_in = [row8(weight_ref.at[j], row) for j in range(4)]
    wy_in = [row8(weight_ref.at[j], row + 1) for j in range(4)]
    wz_in = [row8(weight_ref.at[j], row + 2) for j in range(4)]
    row_x[...] = pick(sub - bx, wx_in)
    along_x = [jnp.broadcast_to(row_x[x : x + 1, :], (8, M)) for x in range(XE)]
    cells_y = [
        sub + 1,
        sub + 9,
        jnp.where(sub < 2, sub + 17, jnp.where(sub == 7, 0, -100)),
    ]
    along_y = [pick(cell - by, wy_in) for cell in cells_y]
    tiles = []
    values = []
    for half in range(2):
        lead = sub - bz + (1 + 8 * half)
        tiles.append(((15 - lead) >> 4).astype(jnp.float32))
        values.append(pick(lead & 15, wz_in))
    tile = jnp.concatenate(tiles, axis=0).astype(jnp.bfloat16)
    return along_x, along_y, tile, values


def expand(tile, value):
    zero = jnp.zeros((16, M), jnp.bfloat16)
    value = jnp.concatenate(value, axis=0).astype(jnp.bfloat16)
    return [jnp.where(tile == r, value, zero) for r in range(NZ // 16)]


def spread_kernel(load_ref, out_ref, base_ref, weight_ref, row_x, total):
    blocks = load_ref.shape[0] // 6
    prepare_weights(load_ref, base_ref, weight_ref)
    total[...] = jnp.zeros_like(total)

    def turn(i, carry):
        planes = []
        loads = []
        for g in range(GROUP):
            row = (i * GROUP + g) * 6
            along_x, along_y, tile, value = block_weights(
                base_ref, weight_ref, row, row_x.at[g]
            )
            loaded = []
            for c in range(3):
                force = row8(load_ref, row + 3 + c)
                loaded += expand(tile, [part * force for part in value])
            loads.append(jnp.concatenate(loaded, axis=0))
            plane = [along_x[x] * along_y[k] for x in range(XE) for k in range(3)]
            plane.append(jnp.zeros((8, M), jnp.float32))
            planes.append(jnp.concatenate(plane, axis=0).astype(jnp.bfloat16))
        total[...] += lax.dot_general(
            jnp.concatenate(loads, axis=1),
            jnp.concatenate(planes, axis=1),
            (((1,), (1,)), ((), ())),
            preferred_element_type=jnp.float32,
        )
        return carry

    lax.fori_loop(0, blocks // GROUP, turn, 0)
    out_ref[...] = jnp.transpose(total[...]).astype(out_ref.dtype)


def join_kernel(mine_ref, other_ref, old_ref, sum_ref, low_ref, high_ref):
    rim = 3 * YP
    sum_ref[...] = 0.5 * (
        mine_ref[0:ROWS, :].astype(jnp.float32) + other_ref[0:ROWS, :].astype(jnp.float32)
    )
    for x in range(4):
        for c in range(3):
            at = (x + 1) * YP
            sum_ref[at : at + 16, c * NZ : (c + 1) * NZ] += old_ref[x, c]
    low_ref[...] = sum_ref[0:rim, :].astype(jnp.bfloat16)
    high_ref[...] = sum_ref[ROWS - rim : ROWS, :].astype(jnp.bfloat16)


HIGH_ROWS = (15, 16, 17)
LOW_ROWS = (23, 0, 1)


def fold_kernel(
    sum_ref, left_ref, right_ref, edge_low_ref, edge_high_ref, out_ref, low_ref, high_ref, low, high
):
    rim = 3 * YP
    out_ref[rim : ROWS - rim, :] = sum_ref[rim : ROWS - rim, :]
    out_ref[0:rim, :] = sum_ref[0:rim, :] + left_ref[...].astype(jnp.float32)
    out_ref[ROWS - rim : ROWS, :] = sum_ref[ROWS - rim : ROWS, :] + right_ref[...].astype(jnp.float32)
    for sent, edge, rows in ((low, edge_low_ref, LOW_ROWS), (high, edge_high_ref, HIGH_ROWS)):
        sent[...] = jnp.zeros_like(sent)
        for x in range(XE):
            for j in range(3):
                at = x * YP + rows[j]
                sent[x * 3 + j : x * 3 + j + 1, :] = out_ref[at : at + 1, :]
        sent[24:32, :] = edge[:, 0 : 3 * NZ]
        sent[32:40, 0 : 2 * NZ] = edge[:, 3 * NZ : 5 * NZ]
    low_ref[...] = low[...].astype(jnp.bfloat16)
    high_ref[...] = high[...].astype(jnp.bfloat16)


def face_flux(before, after):
    flux = []
    thick = 0.25 * (before(4) + after(4))
    for c in range(3):
        flux.append(thick * (after(c) - before(c)))
    return flux, 0.5 * (after(3) - before(3))


def sample_kernel(
    fluid_count,
    sub_count,
    place_ref,
    load_ref,
    sum_ref,
    below_ref,
    above_ref,
    edge_low_ref,
    edge_high_ref,
    fresh_ref,
    out_ref,
    base_ref,
    weight_ref,
    row_x,
    grid,
    field,
    below,
    above,
):
    blocks = load_ref.shape[0] // 6
    prepare_weights(load_ref, base_ref, weight_ref)
    grid[...] = sum_ref[...]
    below[...] = below_ref[...].astype(jnp.float32)
    above[...] = above_ref[...].astype(jnp.float32)
    mine_low = lambda f: edge_low_ref[:, f * NZ : (f + 1) * NZ]
    mine_high = lambda f: edge_high_ref[:, f * NZ : (f + 1) * NZ]

    def theirs(ref):
        return lambda f: (
            ref[24:32, f * NZ : (f + 1) * NZ]
            if f < 3
            else ref[32:40, (f - 3) * NZ : (f - 2) * NZ]
        )

    for come, rows, before, after in (
        (below, LOW_ROWS, theirs(below), mine_low),
        (above, HIGH_ROWS, mine_high, theirs(above)),
    ):
        flux, step = face_flux(before, after)
        plus = jnp.concatenate([flux[0], flux[1] - step, flux[2]], axis=1)
        minus = jnp.concatenate(flux, axis=1)
        for x in range(XE):
            for j in range(3):
                more = come[x * 3 + j : x * 3 + j + 1, :]
                if j == 0:
                    more = more + plus[x : x + 1, :]
                if j == 1:
                    more = more - minus[x : x + 1, :]
                at = x * YP + rows[j]
                grid[at : at + 1, :] += more
    for x in range(4):
        for c in range(3):
            at = (x + 1) * YP
            fresh_ref[x, c] = grid[at : at + 16, c * NZ : (c + 1) * NZ]
    first = place_ref[0]
    second = place_ref[1]
    sub = iota((8, 3 * NZ), 0)
    inside = ((sub < 2) & (second < sub_count - 1)) | ((sub == 7) & (second > 0))
    for x in range(XE):
        at = x * YP + 16
        grid[at : at + 8, :] = jnp.where(inside, grid[at : at + 8, :], 0.0)

    @pl.when(first == 0)
    def _():
        grid[0:YP, :] = jnp.zeros((YP, 3 * NZ), jnp.float32)

    @pl.when(first == fluid_count - 1)
    def _():
        grid[5 * YP : ROWS, :] = jnp.zeros((2 * YP, 3 * NZ), jnp.float32)

    rows = [grid[:, c * NZ : (c + 1) * NZ] for c in range(3)]
    rows.append(jnp.zeros((FIELD - 3 * ROWS, NZ), jnp.float32))
    field[...] = jnp.concatenate(rows, axis=0).astype(jnp.bfloat16)

    def turn(i, carry):
        for t in range(TURNS):
            block = (i * TURNS + t) * PAIR
            parts = []
            depth = []
            for g in range(PAIR):
                along_x, along_y, tile, value = block_weights(
                    base_ref, weight_ref, (block + g) * 6, row_x.at[t * PAIR + g]
                )
                parts.append((along_x, along_y))
                depth.append(jnp.concatenate(expand(tile, value), axis=0))
            seen = lax.dot_general(
                field[...],
                jnp.concatenate(depth, axis=1),
                (((1,), (0,)), ((), ())),
                preferred_element_type=jnp.float32,
            )
            for g in range(PAIR):
                along_x, along_y = parts[g]
                for c in range(3):
                    total = 0.0
                    for k in range(3):
                        inner = 0.0
                        for x in range(XE):
                            at = c * ROWS + x * YP + k * 8
                            inner = inner + along_x[x] * seen[at : at + 8, g * M : (g + 1) * M]
                        total = total + inner * along_y[k]
                    out_ref[pl.ds((block + g) * 3 + c, 1), :] = jnp.sum(
                        total, axis=0, keepdims=True
                    )
        return carry

    lax.fori_loop(0, blocks // (PAIR * TURNS), turn, 0)


def take_kernel(blocks, pos_ref, in_ref, out_ref):
    for b in range(blocks):
        slot = pos_ref[b]
        for c in range(3):
            out_ref[c, b : b + 1, :] = in_ref[pl.ds(slot * 3 + c, 1), :]


def shift(array, axis, by):
    count = lax.axis_size(axis)
    if by > 0:
        pairs = [(i, i + 1) for i in range(count - 1)]
    else:
        pairs = [(i + 1, i) for i in range(count - 1)]
    return lax.ppermute(array, axis, pairs)


def old_kernel(v_ref, p_ref, n_ref, before_ref, after_ref, out_ref, edge_low_ref, edge_high_ref):
    rows, lanes = p_ref.shape[1:]
    y = iota((rows, lanes), 0)
    z = iota((rows, lanes), 1)
    before = [before_ref[0, f].astype(jnp.float32) for f in range(5)]
    after = [[after_ref[x, f].astype(jnp.float32) for f in range(5)] for x in range(2)]
    every = [[v_ref[x, c] for c in range(3)] + [p_ref[x], n_ref[x]] for x in range(4)]
    columns = [before, *every, *after]
    for edge_ref, at in ((edge_low_ref, 0), (edge_high_ref, rows - 1)):
        edge_ref[XE : XE + 1, :] = jnp.zeros((1, 5 * lanes), jnp.float32)
        for x in range(XE):
            for f in range(5):
                edge_ref[x : x + 1, f * lanes : (f + 1) * lanes] = columns[x][f][at : at + 1, :]
    steps = (
        lambda x, f: columns[x + 1][f],
        lambda x, f: columns[x - 1][f],
        lambda x, f: jnp.where(y == rows - 1, columns[x][f], pltpu.roll(columns[x][f], rows - 1, 0)),
        lambda x, f: jnp.where(y == 0, columns[x][f], pltpu.roll(columns[x][f], 1, 0)),
        lambda x, f: jnp.where(z == lanes - 1, 0.0, pltpu.roll(columns[x][f], lanes - 1, 1)),
        lambda x, f: jnp.where(z == 0, 0.0, pltpu.roll(columns[x][f], 1, 1)),
    )
    for x in range(1, 5):
        thick = [0.25 * (columns[x][4] + step(x, 4)) for step in steps]
        for c in range(3):
            here = columns[x][c]
            total = here - 0.5 * (steps[2 * c](x, 3) - columns[x][3])
            for k in range(6):
                total = total + thick[k] * (steps[k](x, c) - here)
            out_ref[x - 1, c] = total


def old_part(velocity, pressure, viscosity):
    v = jnp.transpose(velocity, (0, 2, 1, 3))
    picked = lambda rows: jnp.concatenate(
        [v[rows], pressure[rows][:, None], viscosity[rows][:, None]], axis=1
    ).astype(jnp.bfloat16)
    before = shift(picked(slice(3, 4)), "fluid", 1)
    after = shift(picked(slice(0, 2)), "fluid", -1)
    edge = jax.ShapeDtypeStruct((XE + 1, 5 * NZ), jnp.float32)
    return pl.pallas_call(
        old_kernel,
        out_shape=(jax.ShapeDtypeStruct(v.shape, jnp.float32), edge, edge),
        in_specs=[VMEM] * 5,
        out_specs=(VMEM,) * 3,
        compiler_params=grant(6),
        name="old",
    )(v, pressure, viscosity, before, after)


def grant(mib):
    return pltpu.CompilerParams(vmem_limit_bytes=mib * 1024 * 1024)


def spread(arrived):
    return pl.pallas_call(
        spread_kernel,
        out_shape=jax.ShapeDtypeStruct((ROWS_PAD, 3 * NZ), jnp.bfloat16),
        in_specs=[VMEM],
        out_specs=VMEM,
        scratch_shapes=[
            pltpu.VMEM(arrived.shape, jnp.int32),
            pltpu.VMEM((4, *arrived.shape), jnp.float32),
            pltpu.VMEM((GROUP, 8, M), jnp.float32),
            pltpu.VMEM((3 * NZ, ROWS_PAD), jnp.float32),
        ],
        compiler_params=grant(16),
        name="spread",
    )(arrived)


def sample(slabs, subs, place, arrived, folded, from_below, from_above, edge_low, edge_high):
    lanes = 3 * NZ
    return pl.pallas_call(
        lambda *refs: sample_kernel(slabs, subs, *refs),
        out_shape=(
            jax.ShapeDtypeStruct((4, 3, 16, NZ), jnp.float32),
            jax.ShapeDtypeStruct((arrived.shape[0] // 2, M), jnp.float32),
        ),
        in_specs=[SMEM] + [VMEM] * 6,
        out_specs=(VMEM, VMEM),
        scratch_shapes=[
            pltpu.VMEM(arrived.shape, jnp.int32),
            pltpu.VMEM((4, *arrived.shape), jnp.float32),
            pltpu.VMEM((PAIR * TURNS, 8, M), jnp.float32),
            pltpu.VMEM((ROWS, lanes), jnp.float32),
            pltpu.VMEM((FIELD, NZ), jnp.bfloat16),
            pltpu.VMEM((40, lanes), jnp.float32),
            pltpu.VMEM((40, lanes), jnp.float32),
        ],
        compiler_params=grant(16),
        name="sample",
    )(place, arrived, folded, from_below, from_above, edge_low, edge_high)


def body(velocity, pressure, viscosity, marker_force, marker_offset, cell_base, block_slab):
    f32, bf16 = jnp.float32, jnp.bfloat16
    shape = jax.ShapeDtypeStruct
    blocks = marker_force.shape[0]
    slabs = lax.axis_size("fluid")
    subs = lax.axis_size("sub")
    slots = 2 * slabs
    lanes = 3 * NZ
    swap01 = lambda array: jnp.transpose(array, (1, 0, 2))
    payload, position = pl.pallas_call(
        lambda *refs: pack_kernel(blocks, *refs),
        out_shape=(shape((slots * 6, M), f32), shape((blocks,), jnp.int32)),
        in_specs=[SMEM, VMEM, VMEM, VMEM],
        out_specs=(VMEM, SMEM),
        scratch_shapes=[pltpu.SMEM((slabs,), jnp.int32), pltpu.VMEM((3, blocks, M), f32)],
        compiler_params=grant(60),
        name="pack",
    )(block_slab[:, 0], swap01(marker_offset), swap01(cell_base), swap01(marker_force))
    payload, velocity, pressure, viscosity = lax.optimization_barrier(
        (payload, velocity, pressure, viscosity)
    )
    arrived = lax.all_to_all(
        payload.reshape(slabs, 3, 4, M), "fluid", split_axis=0, concat_axis=0, tiled=True
    ).reshape(slots * 6, M)
    old, edge_low, edge_high = old_part(velocity, pressure, viscosity)
    partial_grid = spread(arrived)
    other_grid = lax.ppermute(partial_grid, "struct", [(0, 1), (1, 0)])
    rim = 3 * YP
    summed, low, high = pl.pallas_call(
        join_kernel,
        out_shape=(shape((ROWS, lanes), f32), shape((rim, lanes), bf16), shape((rim, lanes), bf16)),
        in_specs=[VMEM] * 3,
        out_specs=(VMEM,) * 3,
        compiler_params=grant(6),
        name="join",
    )(partial_grid, other_grid, old)
    from_left = shift(high, "fluid", 1)
    from_right = shift(low, "fluid", -1)
    folded, low, high = pl.pallas_call(
        fold_kernel,
        out_shape=(shape((ROWS, lanes), f32), shape((40, lanes), bf16), shape((40, lanes), bf16)),
        in_specs=[VMEM] * 5,
        out_specs=(VMEM,) * 3,
        scratch_shapes=[pltpu.VMEM((40, lanes), f32)] * 2,
        compiler_params=grant(6),
        name="fold",
    )(summed, from_left, from_right, edge_low, edge_high)
    from_below = shift(high, "sub", 1)
    from_above = shift(low, "sub", -1)
    place = jnp.stack([lax.axis_index("fluid"), lax.axis_index("sub")]).astype(jnp.int32)
    fresh, sampled = sample(
        slabs, subs, place, arrived, folded, from_below, from_above, edge_low, edge_high
    )
    returned = lax.all_to_all(
        sampled.reshape(slabs, 3, 2, M), "fluid", split_axis=0, concat_axis=0, tiled=True
    ).reshape(slots * 3, M)
    result = pl.pallas_call(
        lambda *refs: take_kernel(blocks, *refs),
        out_shape=shape((3, blocks, M), f32),
        in_specs=[SMEM, VMEM],
        out_specs=VMEM,
        compiler_params=grant(2),
        name="take",
    )(position, returned)
    return (jnp.transpose(fresh, (0, 2, 1, 3)), swap01(result))


def solution(mesh):
    return jax.shard_map(
        body,
        mesh=mesh,
        in_specs=(
            P("fluid", "sub", None, None),
            P("fluid", "sub", None),
            P("fluid", "sub", None),
            P(("fluid", "sub", "struct"), None, None),
            P(("fluid", "sub", "struct"), None, None),
            P(("fluid", "sub", "struct"), None, None),
            P(("fluid", "sub", "struct"), None),
        ),
        out_specs=(P("fluid", "sub", None, None), P(("fluid", "sub", "struct"), None, None)),
        check_vma=False,
    )
```

```python
import math

import jax
import jax.numpy as jnp
from jax import lax
from jax.experimental import pallas as pl
from jax.experimental.pallas import tpu as pltpu
from jax.sharding import PartitionSpec as P

M = 128
NZ = 256
YP = 24
XE = 7
ROWS = XE * YP
ROWS_PAD = 176
FIELD = 512
GROUP = 32
PAIR = 2
TURNS = 16

VMEM = pl.BlockSpec(memory_space=pltpu.VMEM)
SMEM = pl.BlockSpec(memory_space=pltpu.SMEM)


def iota(shape, dim):
    return lax.broadcasted_iota(jnp.int32, shape, dim)


def pack_kernel(blocks, slab_ref, offset_ref, base_ref, force_ref, out_ref, pos_ref, count, coords):
    slots = out_ref.shape[0] // 6
    out_ref[...] = jnp.zeros_like(out_ref)
    coords[...] = base_ref[...].astype(jnp.float32) + offset_ref[...]

    for i in range(slots // 2):
        count[i] = 0
    for b in range(blocks):
        slab = slab_ref[b]
        place = count[slab]
        count[slab] = place + 1
        slot = slab * 2 + place
        pos_ref[b] = slot
        for j in range(3):
            out_ref[pl.ds(slot * 6 + j, 1), :] = coords[j, b : b + 1, :]
            out_ref[pl.ds(slot * 6 + 3 + j, 1), :] = force_ref[j, b : b + 1, :]


def prepare_weights(load_ref, base_ref, weight_ref):
    rows = load_ref.shape[0]
    step = math.gcd(rows, 64)

    def turn(i, carry):
        at = pl.ds(pl.multiple_of(i * step, step), step)
        place = load_ref[at, :]
        base = jnp.floor(place)
        part = place - base
        root = jnp.sqrt(1.0 + 4.0 * part * (1.0 - part)) * 0.125
        falling = (3.0 - 2.0 * part) * 0.125
        rising = (1.0 + 2.0 * part) * 0.125
        base_ref[at, :] = base.astype(jnp.int32)
        weight_ref[0, at, :] = falling - root
        weight_ref[1, at, :] = falling + root
        weight_ref[2, at, :] = rising + root
        weight_ref[3, at, :] = rising - root
        return carry

    lax.fori_loop(0, rows // step, turn, 0)


def pick(index, weights):
    out = jnp.where(index == 0, weights[0], 0.0)
    for j in range(1, 4):
        out = jnp.where(index == j, weights[j], out)
    return out


def row8(ref, row):
    return jnp.broadcast_to(ref[pl.ds(row, 1), :], (8, M))


def block_weights(base_ref, weight_ref, row, row_x):
    sub = iota((8, M), 0)
    bx = row8(base_ref, row)
    by = row8(base_ref, row + 1)
    bz = row8(base_ref, row + 2)
    wx_in = [row8(weight_ref.at[j], row) for j in range(4)]
    wy_in = [row8(weight_ref.at[j], row + 1) for j in range(4)]
    wz_in = [row8(weight_ref.at[j], row + 2) for j in range(4)]
    row_x[...] = pick(sub - bx, wx_in)
    along_x = [jnp.broadcast_to(row_x[x : x + 1, :], (8, M)) for x in range(XE)]
    cells_y = [
        sub + 1,
        sub + 9,
        jnp.where(sub < 2, sub + 17, jnp.where(sub == 7, 0, -100)),
    ]
    along_y = [pick(cell - by, wy_in) for cell in cells_y]
    tiles = []
    values = []
    for half in range(2):
        lead = sub - bz + (1 + 8 * half)
        tiles.append(((15 - lead) >> 4).astype(jnp.float32))
        values.append(pick(lead & 15, wz_in))
    tile = jnp.concatenate(tiles, axis=0).astype(jnp.bfloat16)
    return along_x, along_y, tile, values


def expand(tile, value):
    zero = jnp.zeros((16, M), jnp.bfloat16)
    value = jnp.concatenate(value, axis=0).astype(jnp.bfloat16)
    return [jnp.where(tile == r, value, zero) for r in range(NZ // 16)]


def spread_kernel(load_ref, out_ref, base_ref, weight_ref, row_x, total):
    blocks = load_ref.shape[0] // 6
    prepare_weights(load_ref, base_ref, weight_ref)
    total[...] = jnp.zeros_like(total)

    def turn(i, carry):
        planes = []
        loads = []
        for g in range(GROUP):
            row = (i * GROUP + g) * 6
            along_x, along_y, tile, value = block_weights(
                base_ref, weight_ref, row, row_x.at[g]
            )
            loaded = []
            for c in range(3):
                force = row8(load_ref, row + 3 + c)
                loaded += expand(tile, [part * force for part in value])
            loads.append(jnp.concatenate(loaded, axis=0))
            plane = [along_x[x] * along_y[k] for x in range(XE) for k in range(3)]
            plane.append(jnp.zeros((8, M), jnp.float32))
            planes.append(jnp.concatenate(plane, axis=0).astype(jnp.bfloat16))
        total[...] += lax.dot_general(
            jnp.concatenate(loads, axis=1),
            jnp.concatenate(planes, axis=1),
            (((1,), (1,)), ((), ())),
            preferred_element_type=jnp.float32,
        )
        return carry

    lax.fori_loop(0, blocks // GROUP, turn, 0)
    out_ref[...] = jnp.transpose(total[...]).astype(out_ref.dtype)


def join_kernel(mine_ref, other_ref, old_ref, sum_ref, low_ref, high_ref):
    rim = 3 * YP
    sum_ref[...] = 0.5 * (
        mine_ref[0:ROWS, :].astype(jnp.float32) + other_ref[0:ROWS, :].astype(jnp.float32)
    )
    for x in range(4):
        for c in range(3):
            at = (x + 1) * YP
            sum_ref[at : at + 16, c * NZ : (c + 1) * NZ] += old_ref[x, c]
    low_ref[...] = sum_ref[0:rim, :].astype(jnp.bfloat16)
    high_ref[...] = sum_ref[ROWS - rim : ROWS, :].astype(jnp.bfloat16)


HIGH_ROWS = (15, 16, 17)
LOW_ROWS = (23, 0, 1)


def fold_kernel(
    sum_ref, left_ref, right_ref, edge_low_ref, edge_high_ref, out_ref, low_ref, high_ref, low, high
):
    rim = 3 * YP
    out_ref[rim : ROWS - rim, :] = sum_ref[rim : ROWS - rim, :]
    out_ref[0:rim, :] = sum_ref[0:rim, :] + left_ref[...].astype(jnp.float32)
    out_ref[ROWS - rim : ROWS, :] = sum_ref[ROWS - rim : ROWS, :] + right_ref[...].astype(jnp.float32)
    for sent, edge, rows in ((low, edge_low_ref, LOW_ROWS), (high, edge_high_ref, HIGH_ROWS)):
        sent[...] = jnp.zeros_like(sent)
        for x in range(XE):
            for j in range(3):
                at = x * YP + rows[j]
                sent[x * 3 + j : x * 3 + j + 1, :] = out_ref[at : at + 1, :]
        sent[24:32, :] = edge[:, 0 : 3 * NZ]
        sent[32:40, 0 : 2 * NZ] = edge[:, 3 * NZ : 5 * NZ]
    low_ref[...] = low[...].astype(jnp.bfloat16)
    high_ref[...] = high[...].astype(jnp.bfloat16)


def face_flux(before, after):
    flux = []
    thick = 0.25 * (before(4) + after(4))
    for c in range(3):
        flux.append(thick * (after(c) - before(c)))
    return flux, 0.5 * (after(3) - before(3))


def sample_kernel(
    fluid_count,
    sub_count,
    place_ref,
    load_ref,
    sum_ref,
    below_ref,
    above_ref,
    edge_low_ref,
    edge_high_ref,
    fresh_ref,
    out_ref,
    base_ref,
    weight_ref,
    row_x,
    grid,
    field,
    below,
    above,
):
    blocks = load_ref.shape[0] // 6
    prepare_weights(load_ref, base_ref, weight_ref)
    grid[...] = sum_ref[...]
    below[...] = below_ref[...].astype(jnp.float32)
    above[...] = above_ref[...].astype(jnp.float32)
    mine_low = lambda f: edge_low_ref[:, f * NZ : (f + 1) * NZ]
    mine_high = lambda f: edge_high_ref[:, f * NZ : (f + 1) * NZ]

    def theirs(ref):
        return lambda f: (
            ref[24:32, f * NZ : (f + 1) * NZ]
            if f < 3
            else ref[32:40, (f - 3) * NZ : (f - 2) * NZ]
        )

    for come, rows, before, after in (
        (below, LOW_ROWS, theirs(below), mine_low),
        (above, HIGH_ROWS, mine_high, theirs(above)),
    ):
        flux, step = face_flux(before, after)
        plus = jnp.concatenate([flux[0], flux[1] - step, flux[2]], axis=1)
        minus = jnp.concatenate(flux, axis=1)
        for x in range(XE):
            for j in range(3):
                more = come[x * 3 + j : x * 3 + j + 1, :]
                if j == 0:
                    more = more + plus[x : x + 1, :]
                if j == 1:
                    more = more - minus[x : x + 1, :]
                at = x * YP + rows[j]
                grid[at : at + 1, :] += more
    for x in range(4):
        for c in range(3):
            at = (x + 1) * YP
            fresh_ref[x, c] = grid[at : at + 16, c * NZ : (c + 1) * NZ]
    first = place_ref[0]
    second = place_ref[1]
    sub = iota((8, 3 * NZ), 0)
    inside = ((sub < 2) & (second < sub_count - 1)) | ((sub == 7) & (second > 0))
    for x in range(XE):
        at = x * YP + 16
        grid[at : at + 8, :] = jnp.where(inside, grid[at : at + 8, :], 0.0)

    @pl.when(first == 0)
    def _():
        grid[0:YP, :] = jnp.zeros((YP, 3 * NZ), jnp.float32)

    @pl.when(first == fluid_count - 1)
    def _():
        grid[5 * YP : ROWS, :] = jnp.zeros((2 * YP, 3 * NZ), jnp.float32)

    rows = [grid[:, c * NZ : (c + 1) * NZ] for c in range(3)]
    rows.append(jnp.zeros((FIELD - 3 * ROWS, NZ), jnp.float32))
    field[...] = jnp.concatenate(rows, axis=0).astype(jnp.bfloat16)

    def turn(i, carry):
        for t in range(TURNS):
            block = (i * TURNS + t) * PAIR
            parts = []
            depth = []
            for g in range(PAIR):
                along_x, along_y, tile, value = block_weights(
                    base_ref, weight_ref, (block + g) * 6, row_x.at[t * PAIR + g]
                )
                parts.append((along_x, along_y))
                depth.append(jnp.concatenate(expand(tile, value), axis=0))
            seen = lax.dot_general(
                field[...],
                jnp.concatenate(depth, axis=1),
                (((1,), (0,)), ((), ())),
                preferred_element_type=jnp.float32,
            )
            for g in range(PAIR):
                along_x, along_y = parts[g]
                for c in range(3):
                    total = 0.0
                    for k in range(3):
                        inner = 0.0
                        for x in range(XE):
                            at = c * ROWS + x * YP + k * 8
                            inner = inner + along_x[x] * seen[at : at + 8, g * M : (g + 1) * M]
                        total = total + inner * along_y[k]
                    out_ref[pl.ds((block + g) * 3 + c, 1), :] = jnp.sum(
                        total, axis=0, keepdims=True
                    )
        return carry

    lax.fori_loop(0, blocks // (PAIR * TURNS), turn, 0)


def take_kernel(blocks, pos_ref, in_ref, out_ref):
    for b in range(blocks):
        slot = pos_ref[b]
        for c in range(3):
            out_ref[c, b : b + 1, :] = in_ref[pl.ds(slot * 3 + c, 1), :]


def shift(array, axis, by):
    count = lax.axis_size(axis)
    if by > 0:
        pairs = [(i, i + 1) for i in range(count - 1)]
    else:
        pairs = [(i + 1, i) for i in range(count - 1)]
    return lax.ppermute(array, axis, pairs)


def old_kernel(v_ref, p_ref, n_ref, before_ref, after_ref, out_ref, edge_low_ref, edge_high_ref):
    rows, lanes = p_ref.shape[1:]
    y = iota((rows, lanes), 0)
    z = iota((rows, lanes), 1)
    before = [before_ref[0, f].astype(jnp.float32) for f in range(5)]
    after = [[after_ref[x, f].astype(jnp.float32) for f in range(5)] for x in range(2)]
    every = [[v_ref[x, c] for c in range(3)] + [p_ref[x], n_ref[x]] for x in range(4)]
    columns = [before, *every, *after]
    for edge_ref, at in ((edge_low_ref, 0), (edge_high_ref, rows - 1)):
        edge_ref[XE : XE + 1, :] = jnp.zeros((1, 5 * lanes), jnp.float32)
        for x in range(XE):
            for f in range(5):
                edge_ref[x : x + 1, f * lanes : (f + 1) * lanes] = columns[x][f][at : at + 1, :]
    steps = (
        lambda x, f: columns[x + 1][f],
        lambda x, f: columns[x - 1][f],
        lambda x, f: jnp.where(y == rows - 1, columns[x][f], pltpu.roll(columns[x][f], rows - 1, 0)),
        lambda x, f: jnp.where(y == 0, columns[x][f], pltpu.roll(columns[x][f], 1, 0)),
        lambda x, f: jnp.where(z == lanes - 1, 0.0, pltpu.roll(columns[x][f], lanes - 1, 1)),
        lambda x, f: jnp.where(z == 0, 0.0, pltpu.roll(columns[x][f], 1, 1)),
    )
    for x in range(1, 5):
        thick = [0.25 * (columns[x][4] + step(x, 4)) for step in steps]
        for c in range(3):
            here = columns[x][c]
            total = here - 0.5 * (steps[2 * c](x, 3) - columns[x][3])
            for k in range(6):
                total = total + thick[k] * (steps[k](x, c) - here)
            out_ref[x - 1, c] = total


def edge_kernel(v_ref, p_ref, n_ref, first_ref, last_ref):
    for ref, start in ((first_ref, 0), (last_ref, v_ref.shape[0] - 1)):
        for x in range(ref.shape[0]):
            for c in range(3):
                ref[x, c] = v_ref[start + x, c].astype(jnp.bfloat16)
            ref[x, 3] = p_ref[start + x].astype(jnp.bfloat16)
            ref[x, 4] = n_ref[start + x].astype(jnp.bfloat16)


def old_part(velocity, pressure, viscosity):
    v = jnp.transpose(velocity, (0, 2, 1, 3))
    rows = lambda count: jax.ShapeDtypeStruct((count, 5, *v.shape[2:]), jnp.bfloat16)
    first, last = pl.pallas_call(
        edge_kernel,
        out_shape=(rows(2), rows(1)),
        in_specs=[VMEM] * 3,
        out_specs=(VMEM, VMEM),
        compiler_params=grant(50),
        name="edge",
    )(v, pressure, viscosity)
    before = shift(last, "fluid", 1)
    after = shift(first, "fluid", -1)
    edge = jax.ShapeDtypeStruct((XE + 1, 5 * NZ), jnp.float32)
    return pl.pallas_call(
        old_kernel,
        out_shape=(jax.ShapeDtypeStruct(v.shape, jnp.float32), edge, edge),
        in_specs=[VMEM] * 5,
        out_specs=(VMEM,) * 3,
        compiler_params=grant(6),
        name="old",
    )(v, pressure, viscosity, before, after)


def grant(mib):
    return pltpu.CompilerParams(vmem_limit_bytes=mib * 1024 * 1024)


def spread(arrived):
    return pl.pallas_call(
        spread_kernel,
        out_shape=jax.ShapeDtypeStruct((ROWS_PAD, 3 * NZ), jnp.bfloat16),
        in_specs=[VMEM],
        out_specs=VMEM,
        scratch_shapes=[
            pltpu.VMEM(arrived.shape, jnp.int32),
            pltpu.VMEM((4, *arrived.shape), jnp.float32),
            pltpu.VMEM((GROUP, 8, M), jnp.float32),
            pltpu.VMEM((3 * NZ, ROWS_PAD), jnp.float32),
        ],
        compiler_params=grant(16),
        name="spread",
    )(arrived)


def sample(slabs, subs, place, arrived, folded, from_below, from_above, edge_low, edge_high):
    lanes = 3 * NZ
    return pl.pallas_call(
        lambda *refs: sample_kernel(slabs, subs, *refs),
        out_shape=(
            jax.ShapeDtypeStruct((4, 3, 16, NZ), jnp.float32),
            jax.ShapeDtypeStruct((arrived.shape[0] // 2, M), jnp.float32),
        ),
        in_specs=[SMEM] + [VMEM] * 6,
        out_specs=(VMEM, VMEM),
        scratch_shapes=[
            pltpu.VMEM(arrived.shape, jnp.int32),
            pltpu.VMEM((4, *arrived.shape), jnp.float32),
            pltpu.VMEM((PAIR * TURNS, 8, M), jnp.float32),
            pltpu.VMEM((ROWS, lanes), jnp.float32),
            pltpu.VMEM((FIELD, NZ), jnp.bfloat16),
            pltpu.VMEM((40, lanes), jnp.float32),
            pltpu.VMEM((40, lanes), jnp.float32),
        ],
        compiler_params=grant(16),
        name="sample",
    )(place, arrived, folded, from_below, from_above, edge_low, edge_high)


def body(velocity, pressure, viscosity, marker_force, marker_offset, cell_base, block_slab):
    f32, bf16 = jnp.float32, jnp.bfloat16
    shape = jax.ShapeDtypeStruct
    blocks = marker_force.shape[0]
    slabs = lax.axis_size("fluid")
    subs = lax.axis_size("sub")
    slots = 2 * slabs
    lanes = 3 * NZ
    swap01 = lambda array: jnp.transpose(array, (1, 0, 2))
    payload, position = pl.pallas_call(
        lambda *refs: pack_kernel(blocks, *refs),
        out_shape=(shape((slots * 6, M), f32), shape((blocks,), jnp.int32)),
        in_specs=[SMEM, VMEM, VMEM, VMEM],
        out_specs=(VMEM, SMEM),
        scratch_shapes=[pltpu.SMEM((slabs,), jnp.int32), pltpu.VMEM((3, blocks, M), f32)],
        compiler_params=grant(60),
        name="pack",
    )(block_slab[:, 0], swap01(marker_offset), swap01(cell_base), swap01(marker_force))
    arrived = lax.all_to_all(
        payload.reshape(slabs, 3, 4, M), "fluid", split_axis=0, concat_axis=0, tiled=True
    ).reshape(slots * 6, M)
    old, edge_low, edge_high = old_part(velocity, pressure, viscosity)
    partial_grid = spread(arrived)
    other_grid = lax.ppermute(partial_grid, "struct", [(0, 1), (1, 0)])
    rim = 3 * YP
    summed, low, high = pl.pallas_call(
        join_kernel,
        out_shape=(shape((ROWS, lanes), f32), shape((rim, lanes), bf16), shape((rim, lanes), bf16)),
        in_specs=[VMEM] * 3,
        out_specs=(VMEM,) * 3,
        compiler_params=grant(6),
        name="join",
    )(partial_grid, other_grid, old)
    from_left = shift(high, "fluid", 1)
    from_right = shift(low, "fluid", -1)
    folded, low, high = pl.pallas_call(
        fold_kernel,
        out_shape=(shape((ROWS, lanes), f32), shape((40, lanes), bf16), shape((40, lanes), bf16)),
        in_specs=[VMEM] * 5,
        out_specs=(VMEM,) * 3,
        scratch_shapes=[pltpu.VMEM((40, lanes), f32)] * 2,
        compiler_params=grant(6),
        name="fold",
    )(summed, from_left, from_right, edge_low, edge_high)
    from_below = shift(high, "sub", 1)
    from_above = shift(low, "sub", -1)
    place = jnp.stack([lax.axis_index("fluid"), lax.axis_index("sub")]).astype(jnp.int32)
    fresh, sampled = sample(
        slabs, subs, place, arrived, folded, from_below, from_above, edge_low, edge_high
    )
    returned = lax.all_to_all(
        sampled.reshape(slabs, 3, 2, M), "fluid", split_axis=0, concat_axis=0, tiled=True
    ).reshape(slots * 3, M)
    result = pl.pallas_call(
        lambda *refs: take_kernel(blocks, *refs),
        out_shape=shape((3, blocks, M), f32),
        in_specs=[SMEM, VMEM],
        out_specs=VMEM,
        compiler_params=grant(2),
        name="take",
    )(position, returned)
    return (jnp.transpose(fresh, (0, 2, 1, 3)), swap01(result))


def solution(mesh):
    return jax.shard_map(
        body,
        mesh=mesh,
        in_specs=(
            P("fluid", "sub", None, None),
            P("fluid", "sub", None),
            P("fluid", "sub", None),
            P(("fluid", "sub", "struct"), None, None),
            P(("fluid", "sub", "struct"), None, None),
            P(("fluid", "sub", "struct"), None, None),
            P(("fluid", "sub", "struct"), None),
        ),
        out_specs=(P("fluid", "sub", None, None), P(("fluid", "sub", "struct"), None, None)),
        check_vma=False,
    )
```

```python
import math

import jax
import jax.numpy as jnp
from jax import lax
from jax.experimental import pallas as pl
from jax.experimental.pallas import tpu as pltpu
from jax.sharding import PartitionSpec as P

M = 128
NZ = 256
YP = 24
XE = 7
ROWS = XE * YP
ROWS_PAD = 176
FIELD = 512
GROUP = 128
PAIR = 2
TURNS = 64

VMEM = pl.BlockSpec(memory_space=pltpu.VMEM)
SMEM = pl.BlockSpec(memory_space=pltpu.SMEM)
HBM = pl.BlockSpec(memory_space=pltpu.HBM)


def iota(shape, dim):
    return lax.broadcasted_iota(jnp.int32, shape, dim)


def pack_kernel(
    slab_hbm, offset_hbm, base_hbm, force_hbm, out_ref, slab_ref, offset_ref, base_ref, force_ref, count, sems
):
    copies = [
        pltpu.make_async_copy(source, target, sems.at[k])
        for k, (source, target) in enumerate(
            (
                (slab_hbm, slab_ref),
                (offset_hbm, offset_ref),
                (base_hbm, base_ref),
                (force_hbm, force_ref),
            )
        )
    ]
    for copy in copies:
        copy.start()
    out_ref[...] = jnp.zeros_like(out_ref)
    for i in range(out_ref.shape[0] // 12):
        count[i] = 0
    for copy in copies:
        copy.wait()
    offset_ref[...] = base_ref[...].astype(jnp.float32) + offset_ref[...]
    for b in range(slab_ref.shape[0]):
        slab = slab_ref[b]
        place = count[slab]
        count[slab] = place + 1
        slot = slab * 2 + place
        for j in range(3):
            out_ref[pl.ds(slot * 6 + j, 1), :] = offset_ref[j, b : b + 1, :]
            out_ref[pl.ds(slot * 6 + 3 + j, 1), :] = force_ref[j, b : b + 1, :]


def find_kernel(slab_ref, pos_ref, count):
    for i in range(count.shape[0]):
        count[i] = 0
    for b in range(slab_ref.shape[0]):
        slab = slab_ref[b]
        place = count[slab]
        count[slab] = place + 1
        pos_ref[b] = slab * 2 + place


def prepare_weights(load_ref, base_ref, weight_ref):
    rows = load_ref.shape[0]
    step = math.gcd(rows, 64)

    def turn(i, carry):
        at = pl.ds(pl.multiple_of(i * step, step), step)
        place = load_ref[at, :]
        base = jnp.floor(place)
        part = place - base
        root = jnp.sqrt(1.0 + 4.0 * part * (1.0 - part)) * 0.125
        falling = (3.0 - 2.0 * part) * 0.125
        rising = (1.0 + 2.0 * part) * 0.125
        base_ref[at, :] = base.astype(jnp.int32)
        weight_ref[0, at, :] = falling - root
        weight_ref[1, at, :] = falling + root
        weight_ref[2, at, :] = rising + root
        weight_ref[3, at, :] = rising - root
        return carry

    lax.fori_loop(0, rows // step, turn, 0)


def pick(index, weights):
    out = jnp.where(index == 0, weights[0], 0.0)
    for j in range(1, 4):
        out = jnp.where(index == j, weights[j], out)
    return out


def row8(ref, row):
    return jnp.broadcast_to(ref[pl.ds(row, 1), :], (8, M))


def block_weights(base_ref, weight_ref, row, row_x):
    sub = iota((8, M), 0)
    bx = row8(base_ref, row)
    by = row8(base_ref, row + 1)
    bz = row8(base_ref, row + 2)
    wx_in = [row8(weight_ref.at[j], row) for j in range(4)]
    wy_in = [row8(weight_ref.at[j], row + 1) for j in range(4)]
    wz_in = [row8(weight_ref.at[j], row + 2) for j in range(4)]
    row_x[...] = pick(sub - bx, wx_in)
    along_x = [jnp.broadcast_to(row_x[x : x + 1, :], (8, M)) for x in range(XE)]
    cells_y = [
        sub + 1,
        sub + 9,
        jnp.where(sub < 2, sub + 17, jnp.where(sub == 7, 0, -100)),
    ]
    along_y = [pick(cell - by, wy_in) for cell in cells_y]
    tiles = []
    values = []
    for half in range(2):
        lead = sub - bz + (1 + 8 * half)
        tiles.append(((15 - lead) >> 4).astype(jnp.float32))
        values.append(pick(lead & 15, wz_in))
    tile = jnp.concatenate(tiles, axis=0).astype(jnp.bfloat16)
    return along_x, along_y, tile, values


def expand(tile, value):
    zero = jnp.zeros((16, M), jnp.bfloat16)
    value = jnp.concatenate(value, axis=0).astype(jnp.bfloat16)
    return [jnp.where(tile == r, value, zero) for r in range(NZ // 16)]


def spread_kernel(load_ref, out_ref, base_ref, weight_ref, row_x, total):
    blocks = load_ref.shape[0] // 6
    prepare_weights(load_ref, base_ref, weight_ref)
    total[...] = jnp.zeros_like(total)

    def turn(i, carry):
        planes = []
        loads = []
        for g in range(GROUP):
            row = (i * GROUP + g) * 6
            along_x, along_y, tile, value = block_weights(
                base_ref, weight_ref, row, row_x.at[g]
            )
            loaded = []
            for c in range(3):
                force = row8(load_ref, row + 3 + c)
                loaded += expand(tile, [part * force for part in value])
            loads.append(jnp.concatenate(loaded, axis=0))
            plane = [along_x[x] * along_y[k] for x in range(XE) for k in range(3)]
            plane.append(jnp.zeros((8, M), jnp.float32))
            planes.append(jnp.concatenate(plane, axis=0).astype(jnp.bfloat16))
        total[...] += lax.dot_general(
            jnp.concatenate(loads, axis=1),
            jnp.concatenate(planes, axis=1),
            (((1,), (1,)), ((), ())),
            preferred_element_type=jnp.float32,
        )
        return carry

    lax.fori_loop(0, blocks // GROUP, turn, 0)
    out_ref[...] = jnp.transpose(total[...]).astype(out_ref.dtype)


def join_kernel(mine_ref, other_ref, old_ref, sum_ref, low_ref, high_ref):
    rim = 3 * YP
    sum_ref[...] = 0.5 * (
        mine_ref[0:ROWS, :].astype(jnp.float32) + other_ref[0:ROWS, :].astype(jnp.float32)
    )
    for x in range(4):
        for c in range(3):
            at = (x + 1) * YP
            sum_ref[at : at + 16, c * NZ : (c + 1) * NZ] += old_ref[x, c]
    low_ref[...] = sum_ref[0:rim, :].astype(jnp.bfloat16)
    high_ref[...] = sum_ref[ROWS - rim : ROWS, :].astype(jnp.bfloat16)


HIGH_ROWS = (15, 16, 17)
LOW_ROWS = (23, 0, 1)


def fold_kernel(
    sum_ref, left_ref, right_ref, edge_low_ref, edge_high_ref, out_ref, low_ref, high_ref, low, high
):
    rim = 3 * YP
    out_ref[rim : ROWS - rim, :] = sum_ref[rim : ROWS - rim, :]
    out_ref[0:rim, :] = sum_ref[0:rim, :] + left_ref[...].astype(jnp.float32)
    out_ref[ROWS - rim : ROWS, :] = sum_ref[ROWS - rim : ROWS, :] + right_ref[...].astype(jnp.float32)
    for sent, edge, rows in ((low, edge_low_ref, LOW_ROWS), (high, edge_high_ref, HIGH_ROWS)):
        sent[...] = jnp.zeros_like(sent)
        for x in range(XE):
            for j in range(3):
                at = x * YP + rows[j]
                sent[x * 3 + j : x * 3 + j + 1, :] = out_ref[at : at + 1, :]
        sent[24:32, :] = edge[:, 0 : 3 * NZ]
        sent[32:40, 0 : 2 * NZ] = edge[:, 3 * NZ : 5 * NZ]
    low_ref[...] = low[...].astype(jnp.bfloat16)
    high_ref[...] = high[...].astype(jnp.bfloat16)


def face_flux(before, after):
    flux = []
    thick = 0.25 * (before(4) + after(4))
    for c in range(3):
        flux.append(thick * (after(c) - before(c)))
    return flux, 0.5 * (after(3) - before(3))


def sample_kernel(
    fluid_count,
    sub_count,
    place_ref,
    base_ref,
    weight_ref,
    sum_ref,
    below_ref,
    above_ref,
    edge_low_ref,
    edge_high_ref,
    fresh_ref,
    out_ref,
    row_x,
    grid,
    field,
    below,
    above,
):
    blocks = base_ref.shape[0] // 6
    grid[...] = sum_ref[...]
    below[...] = below_ref[...].astype(jnp.float32)
    above[...] = above_ref[...].astype(jnp.float32)
    mine_low = lambda f: edge_low_ref[:, f * NZ : (f + 1) * NZ]
    mine_high = lambda f: edge_high_ref[:, f * NZ : (f + 1) * NZ]

    def theirs(ref):
        return lambda f: (
            ref[24:32, f * NZ : (f + 1) * NZ]
            if f < 3
            else ref[32:40, (f - 3) * NZ : (f - 2) * NZ]
        )

    for come, rows, before, after in (
        (below, LOW_ROWS, theirs(below), mine_low),
        (above, HIGH_ROWS, mine_high, theirs(above)),
    ):
        flux, step = face_flux(before, after)
        plus = jnp.concatenate([flux[0], flux[1] - step, flux[2]], axis=1)
        minus = jnp.concatenate(flux, axis=1)
        for x in range(XE):
            for j in range(3):
                more = come[x * 3 + j : x * 3 + j + 1, :]
                if j == 0:
                    more = more + plus[x : x + 1, :]
                if j == 1:
                    more = more - minus[x : x + 1, :]
                at = x * YP + rows[j]
                grid[at : at + 1, :] += more
    for x in range(4):
        for c in range(3):
            at = (x + 1) * YP
            fresh_ref[x, c] = grid[at : at + 16, c * NZ : (c + 1) * NZ]
    first = place_ref[0]
    second = place_ref[1]
    sub = iota((8, 3 * NZ), 0)
    inside = ((sub < 2) & (second < sub_count - 1)) | ((sub == 7) & (second > 0))
    for x in range(XE):
        at = x * YP + 16
        grid[at : at + 8, :] = jnp.where(inside, grid[at : at + 8, :], 0.0)

    @pl.when(first == 0)
    def _():
        grid[0:YP, :] = jnp.zeros((YP, 3 * NZ), jnp.float32)

    @pl.when(first == fluid_count - 1)
    def _():
        grid[5 * YP : ROWS, :] = jnp.zeros((2 * YP, 3 * NZ), jnp.float32)

    rows = [grid[:, c * NZ : (c + 1) * NZ] for c in range(3)]
    rows.append(jnp.zeros((FIELD - 3 * ROWS, NZ), jnp.float32))
    field[...] = jnp.concatenate(rows, axis=0).astype(jnp.bfloat16)

    def turn(i, carry):
        for t in range(TURNS):
            block = (i * TURNS + t) * PAIR
            parts = []
            depth = []
            for g in range(PAIR):
                along_x, along_y, tile, value = block_weights(
                    base_ref, weight_ref, (block + g) * 6, row_x.at[t * PAIR + g]
                )
                parts.append((along_x, along_y))
                depth.append(jnp.concatenate(expand(tile, value), axis=0))
            seen = lax.dot_general(
                field[...],
                jnp.concatenate(depth, axis=1),
                (((1,), (0,)), ((), ())),
                preferred_element_type=jnp.float32,
            )
            for g in range(PAIR):
                along_x, along_y = parts[g]
                for c in range(3):
                    total = 0.0
                    for k in range(3):
                        inner = 0.0
                        for x in range(XE):
                            at = c * ROWS + x * YP + k * 8
                            inner = inner + along_x[x] * seen[at : at + 8, g * M : (g + 1) * M]
                        total = total + inner * along_y[k]
                    out_ref[pl.ds((block + g) * 3 + c, 1), :] = jnp.sum(
                        total, axis=0, keepdims=True
                    )
        return carry

    lax.fori_loop(0, blocks // (PAIR * TURNS), turn, 0)


def take_kernel(blocks, pos_ref, in_ref, out_ref):
    for b in range(blocks):
        slot = pos_ref[b]
        for c in range(3):
            out_ref[c, b : b + 1, :] = in_ref[pl.ds(slot * 3 + c, 1), :]


def shift(array, axis, by):
    count = lax.axis_size(axis)
    if by > 0:
        pairs = [(i, i + 1) for i in range(count - 1)]
    else:
        pairs = [(i + 1, i) for i in range(count - 1)]
    return lax.ppermute(array, axis, pairs)


def old_kernel(v_ref, p_ref, n_ref, before_ref, after_ref, out_ref, edge_low_ref, edge_high_ref):
    rows, lanes = p_ref.shape[1:]
    y = iota((rows, lanes), 0)
    z = iota((rows, lanes), 1)
    before = [before_ref[0, f].astype(jnp.float32) for f in range(5)]
    after = [[after_ref[x, f].astype(jnp.float32) for f in range(5)] for x in range(2)]
    every = [[v_ref[x, c] for c in range(3)] + [p_ref[x], n_ref[x]] for x in range(4)]
    columns = [before, *every, *after]
    for edge_ref, at in ((edge_low_ref, 0), (edge_high_ref, rows - 1)):
        edge_ref[XE : XE + 1, :] = jnp.zeros((1, 5 * lanes), jnp.float32)
        for x in range(XE):
            for f in range(5):
                edge_ref[x : x + 1, f * lanes : (f + 1) * lanes] = columns[x][f][at : at + 1, :]
    steps = (
        lambda x, f: columns[x + 1][f],
        lambda x, f: columns[x - 1][f],
        lambda x, f: jnp.where(y == rows - 1, columns[x][f], pltpu.roll(columns[x][f], rows - 1, 0)),
        lambda x, f: jnp.where(y == 0, columns[x][f], pltpu.roll(columns[x][f], 1, 0)),
        lambda x, f: jnp.where(z == lanes - 1, 0.0, pltpu.roll(columns[x][f], lanes - 1, 1)),
        lambda x, f: jnp.where(z == 0, 0.0, pltpu.roll(columns[x][f], 1, 1)),
    )
    for x in range(1, 5):
        thick = [0.25 * (columns[x][4] + step(x, 4)) for step in steps]
        for c in range(3):
            here = columns[x][c]
            total = here - 0.5 * (steps[2 * c](x, 3) - columns[x][3])
            for k in range(6):
                total = total + thick[k] * (steps[k](x, c) - here)
            out_ref[x - 1, c] = total


def edge_kernel(v_ref, p_ref, n_ref, first_ref, last_ref):
    for ref, start in ((first_ref, 0), (last_ref, v_ref.shape[0] - 1)):
        for x in range(ref.shape[0]):
            for c in range(3):
                ref[x, c] = v_ref[start + x, c].astype(jnp.bfloat16)
            ref[x, 3] = p_ref[start + x].astype(jnp.bfloat16)
            ref[x, 4] = n_ref[start + x].astype(jnp.bfloat16)


def old_part(velocity, pressure, viscosity):
    v = jnp.transpose(velocity, (0, 2, 1, 3))
    rows = lambda count: jax.ShapeDtypeStruct((count, 5, *v.shape[2:]), jnp.bfloat16)
    first, last = pl.pallas_call(
        edge_kernel,
        out_shape=(rows(2), rows(1)),
        in_specs=[VMEM] * 3,
        out_specs=(VMEM, VMEM),
        compiler_params=grant(50),
        name="edge",
    )(v, pressure, viscosity)
    before = shift(last, "fluid", 1)
    after = shift(first, "fluid", -1)
    edge = jax.ShapeDtypeStruct((XE + 1, 5 * NZ), jnp.float32)
    return pl.pallas_call(
        old_kernel,
        out_shape=(jax.ShapeDtypeStruct(v.shape, jnp.float32), edge, edge),
        in_specs=[VMEM] * 5,
        out_specs=(VMEM,) * 3,
        compiler_params=grant(6),
        name="old",
    )(v, pressure, viscosity, before, after)


def grant(mib):
    return pltpu.CompilerParams(vmem_limit_bytes=mib * 1024 * 1024)


def spread(arrived):
    rows = arrived.shape[0]
    return pl.pallas_call(
        spread_kernel,
        out_shape=(
            jax.ShapeDtypeStruct((ROWS_PAD, 3 * NZ), jnp.bfloat16),
            jax.ShapeDtypeStruct((rows, M), jnp.int32),
            jax.ShapeDtypeStruct((4, rows, M), jnp.float32),
        ),
        in_specs=[VMEM],
        out_specs=(VMEM,) * 3,
        scratch_shapes=[
            pltpu.VMEM((GROUP, 8, M), jnp.float32),
            pltpu.VMEM((3 * NZ, ROWS_PAD), jnp.float32),
        ],
        compiler_params=grant(16),
        name="spread",
    )(arrived)


def sample(slabs, subs, place, base, weight, *grids):
    lanes = 3 * NZ
    return pl.pallas_call(
        lambda *refs: sample_kernel(slabs, subs, *refs),
        out_shape=(
            jax.ShapeDtypeStruct((4, 3, 16, NZ), jnp.float32),
            jax.ShapeDtypeStruct((base.shape[0] // 2, M), jnp.float32),
        ),
        in_specs=[SMEM] + [VMEM] * 7,
        out_specs=(VMEM, VMEM),
        scratch_shapes=[
            pltpu.VMEM((PAIR * TURNS, 8, M), jnp.float32),
            pltpu.VMEM((ROWS, lanes), jnp.float32),
            pltpu.VMEM((FIELD, NZ), jnp.bfloat16),
            pltpu.VMEM((40, lanes), jnp.float32),
            pltpu.VMEM((40, lanes), jnp.float32),
        ],
        compiler_params=grant(16),
        name="sample",
    )(place, base, weight, *grids)


def body(velocity, pressure, viscosity, marker_force, marker_offset, cell_base, block_slab):
    f32, bf16 = jnp.float32, jnp.bfloat16
    shape = jax.ShapeDtypeStruct
    blocks = marker_force.shape[0]
    slabs = lax.axis_size("fluid")
    subs = lax.axis_size("sub")
    slots = 2 * slabs
    lanes = 3 * NZ
    swap01 = lambda array: jnp.transpose(array, (1, 0, 2))
    payload = pl.pallas_call(
        pack_kernel,
        out_shape=shape((slots * 6, M), f32),
        in_specs=[HBM] * 4,
        out_specs=VMEM,
        scratch_shapes=[
            pltpu.SMEM((blocks,), jnp.int32),
            pltpu.VMEM((3, blocks, M), f32),
            pltpu.VMEM((3, blocks, M), jnp.int32),
            pltpu.VMEM((3, blocks, M), f32),
            pltpu.SMEM((slabs,), jnp.int32),
            pltpu.SemaphoreType.DMA((4,)),
        ],
        compiler_params=grant(60),
        name="pack",
    )(block_slab[:, 0], swap01(marker_offset), swap01(cell_base), swap01(marker_force))
    position = pl.pallas_call(
        find_kernel,
        out_shape=shape((blocks,), jnp.int32),
        in_specs=[SMEM],
        out_specs=SMEM,
        scratch_shapes=[pltpu.SMEM((slabs,), jnp.int32)],
        compiler_params=grant(2),
        name="find",
    )(block_slab[:, 0])
    arrived = lax.all_to_all(
        payload.reshape(slabs, 3, 4, M), "fluid", split_axis=0, concat_axis=0, tiled=True
    ).reshape(slots * 6, M)
    old, edge_low, edge_high = old_part(velocity, pressure, viscosity)
    partial_grid, base, weight = spread(arrived)
    other_grid = lax.ppermute(partial_grid, "struct", [(0, 1), (1, 0)])
    rim = 3 * YP
    summed, low, high = pl.pallas_call(
        join_kernel,
        out_shape=(shape((ROWS, lanes), f32), shape((rim, lanes), bf16), shape((rim, lanes), bf16)),
        in_specs=[VMEM] * 3,
        out_specs=(VMEM,) * 3,
        compiler_params=grant(6),
        name="join",
    )(partial_grid, other_grid, old)
    from_left = shift(high, "fluid", 1)
    from_right = shift(low, "fluid", -1)
    folded, low, high = pl.pallas_call(
        fold_kernel,
        out_shape=(shape((ROWS, lanes), f32), shape((40, lanes), bf16), shape((40, lanes), bf16)),
        in_specs=[VMEM] * 5,
        out_specs=(VMEM,) * 3,
        scratch_shapes=[pltpu.VMEM((40, lanes), f32)] * 2,
        compiler_params=grant(6),
        name="fold",
    )(summed, from_left, from_right, edge_low, edge_high)
    from_below = shift(high, "sub", 1)
    from_above = shift(low, "sub", -1)
    place = jnp.stack([lax.axis_index("fluid"), lax.axis_index("sub")]).astype(jnp.int32)
    fresh, sampled = sample(
        slabs, subs, place, base, weight, folded, from_below, from_above, edge_low, edge_high
    )
    returned = lax.all_to_all(
        sampled.reshape(slabs, 3, 2, M), "fluid", split_axis=0, concat_axis=0, tiled=True
    ).reshape(slots * 3, M)
    result = pl.pallas_call(
        lambda *refs: take_kernel(blocks, *refs),
        out_shape=shape((3, blocks, M), f32),
        in_specs=[SMEM, VMEM],
        out_specs=VMEM,
        compiler_params=grant(2),
        name="take",
    )(position, returned)
    return (jnp.transpose(fresh, (0, 2, 1, 3)), swap01(result))


def solution(mesh):
    return jax.shard_map(
        body,
        mesh=mesh,
        in_specs=(
            P("fluid", "sub", None, None),
            P("fluid", "sub", None),
            P("fluid", "sub", None),
            P(("fluid", "sub", "struct"), None, None),
            P(("fluid", "sub", "struct"), None, None),
            P(("fluid", "sub", "struct"), None, None),
            P(("fluid", "sub", "struct"), None),
        ),
        out_specs=(P("fluid", "sub", None, None), P(("fluid", "sub", "struct"), None, None)),
        check_vma=False,
    )
```
